32 devices in a mesh: row: 8 (over y, x, core), col: 4 (over z).
Axes of the slice: x: 2, y: 2, z: 4, core: 2. Of those that a mesh axis runs over, the one named last changes fastest.
Arguments:
- inverse_rows: float32 [16384, 16384], P('col', 'row'), may hold values from -0.5 to 0.5
- panels: float32 [4, 16384, 256], P('col', 'row'), may hold values from -0.75 to 0.75
- diag_inverse: float32 [2, 256, 256], replicated, may hold values from -12 to 12
- pattern: int32 [2, 64], replicated, may hold values 0 or 1
- owner_slot: int32 [2], replicated, may hold values from 0 to 3, as said below
Outputs:
- inverse_column: float32 [2, 16384, 256], P(None, 'row')
- inverse_row: float32 [2, 256, 16384], P(None, None, 'col')
- diag_block: float32 [2, 256, 256], replicated
The draws below stay inside these ranges and needn't reach their ends.
Inputs may be any that keep to these rules, and one draw needn't show every extreme that they name: `owner_slot`: the two supernodes' panels lie in two different slots, one of them the last slot.
All inputs are finite; a program needn't handle non-finite values.
Results may differ from the reference program's by a relative error of at most 0.0001.
Values sent between devices are 32-bit elements; how exact they have to be, the bound alone decides.
A program may use at most 128 MiB of HBM per device.

```python
import jax
import jax.numpy as jnp
from jax import lax

W = 256
BLOCKS = 64
M = 16384
SLOTS = 4


def draw_owner_slot(key, part):
    first_key = jax.random.fold_in(key, 11)
    second_key = jax.random.fold_in(key, 23)
    other = jax.random.randint(first_key, (), 0, SLOTS - 1).astype(jnp.int32)
    flip = jax.random.randint(second_key, (), 0, 2).astype(jnp.int32)
    last = jnp.int32(SLOTS - 1)
    return jnp.where(flip == 1, jnp.stack([last, other]), jnp.stack([other, last])).astype(jnp.int32)


def touch_ends(result, stream_key, least, high):
    dims = result.shape
    index_at = [jax.random.randint(jax.random.fold_in(stream_key, axis), (), 0, dims[axis]) for axis in range(len(dims))]
    result = result.at[tuple(index_at)].set(least)
    longest = dims.index(max(dims))
    index_at[longest] = (index_at[longest] + 1) % dims[longest]
    return result.at[tuple(index_at)].set(high)


def raised(values, key, source, target, blocks, factor):
    owner, partner = [(jnp.arange(values.shape[dim]) // (values.shape[dim] // blocks)).reshape([-1 if axis == dim else 1 for axis in range(values.ndim)]) for dim in (source, target)]
    chosen = jax.random.permutation(key, blocks)[partner]
    strong = (owner == chosen) | (owner == (partner + blocks // 2) % blocks)
    return jnp.where(strong, factor * values, values)


def block_levels(key, shape, shards, smallest, largest):
    factor_of, own = 1.0, jax.random.fold_in(key, 6)
    for dim, shards_of in shards:
        draws = jnp.exp(jax.random.uniform(jax.random.fold_in(own, dim), (shards_of,), jnp.float32, smallest / len(shards), largest / len(shards)))
        factor_of = factor_of * jnp.repeat(draws, shape[dim] // shards_of).reshape([-1 if axis == dim else 1 for axis in range(len(shape))])
    return factor_of


def bell_draw(own_key, extent, scale, reach, shards=(), dtype=jnp.bfloat16):
    array = scale * jax.random.normal(own_key, extent, jnp.float32)
    if shards:
        array = array * block_levels(own_key, extent, shards, -0.22, 0.18)
    return jnp.clip(array, -reach, reach).astype(dtype)


def bell_draw_with(own_key, shape, scale, limit, cuts, heavy, dtype=jnp.bfloat16):
    values = scale * jax.random.normal(own_key, shape, jnp.float32)
    if cuts:
        values = values * block_levels(own_key, shape, cuts, -0.22, 0.18)
    return jnp.clip(raised(values, jax.random.fold_in(own_key, 3), *heavy), -limit, limit).astype(dtype)


def setup_inputs(seed: int = 0) -> dict:
    keys = jax.random.split(jax.random.key(seed), 6)
    return {
        "inverse_rows": bell_draw_with(keys[0], (M, M), (M // 64) ** -0.5, 0.5, ((0, 4), (1, 8)), (1, 0, 8, 2.0), jnp.float32),
        "panels": bell_draw(keys[1], (SLOTS, M, W), 0.125, 0.75, ((0, 4), (1, 8)), jnp.float32),
        "diag_inverse": bell_draw(keys[2], (2, W, W), 2.0, 12.0, (), jnp.float32),
        "pattern": touch_ends((jax.random.randint(keys[3], (2, BLOCKS), 0, 3) < 2).astype(jnp.int32), jax.random.fold_in(keys[3], 1), 0, 1),
        "owner_slot": draw_owner_slot(jax.random.fold_in(keys[5], 71), 0),
    }


def reference(inverse_rows, panels, diag_inverse, pattern, owner_slot):
    columns = []
    transposed = []
    diagonals = []
    for number in range(2):
        rowmask = jnp.repeat(pattern[number].astype(jnp.float32), W)
        chosen = lax.dynamic_index_in_dim(panels, owner_slot[number].astype(jnp.int32), 0, keepdims=False)
        masked = rowmask[:, None] * chosen
        product = jnp.dot(inverse_rows, masked, precision=lax.Precision.HIGHEST, preferred_element_type=jnp.float32)
        column = -(rowmask[:, None] * product)
        columns.append(column)
        transposed.append(column.T)
        inner = jnp.dot(masked.T, column, precision=lax.Precision.HIGHEST, preferred_element_type=jnp.float32)
        diagonals.append(diag_inverse[number] - inner)
    return jnp.stack(columns), jnp.stack(transposed), jnp.stack(diagonals)
```

```python
import functools

import jax
import jax.numpy as jnp
from jax import lax
from jax.experimental import pallas as pl
from jax.experimental.pallas import tpu as pltpu
from jax.sharding import PartitionSpec as P

MESH = pl.DeviceIdType.MESH
F32 = jnp.float32
BF16 = jnp.bfloat16
AHEAD = 2
LAG = 3
ABUF = 4


def halves(x):
    high = x.astype(BF16)
    return high, (x - high.astype(F32)).astype(BF16)


def dot3(a, b, dims=(((1,), (0,)), ((), ()))):
    (ah, al), (bh, bl) = a, b
    dot = functools.partial(lax.dot_general, dimension_numbers=dims, preferred_element_type=F32)
    return dot(ah, bh) + dot(ah, bl) + dot(al, bh)


def kernel(
    n_rows, n_cols,
    a_ref, panel, scale_ref, sign_ref,
    y_out, low_out, diag_out,
    bh, bl, lead, plus, minus, part, y, low, zbuf, abuf, turned, dpart, dbuf, dsum, *rest,
):
    bits = n_rows.bit_length() - 1
    rs_buf = rest[:bits]
    (lead_s, lead_r, plus_s, plus_r, minus_s, minus_r, rs_s, rs_r, ag_s, ag_r,
     zl_s, zr_s, z_r, dl_s, low_r, da_s, da_r, db_s, db_r, a_sem, t_sem, o_sem) = rest[bits:]
    r = lax.axis_index("row")
    c = lax.axis_index("col")
    width = bh.shape[2]
    depth = bh.shape[1]
    rows = y.shape[1]
    end = n_cols - 1
    core = lax.rem(r, 2)
    left, right = {"col": c - 1}, {"col": c + 1}
    strip = rows // 4
    kc = abuf.shape[2]
    ch = kc // 4
    n_ch = depth // ch
    sub = zbuf.shape[3]
    n_sub = zbuf.shape[1]
    piece = strip >> (bits - 1)
    per = piece // sub

    def bit_of(j):
        if j == 0:
            return 1
        return (1 << j) + core * ((1 << (bits - j)) - (1 << j))

    value = [lax.rem(lax.div(r, bit_of(j)), 2) for j in range(bits)]
    partner = [r + (1 - 2 * value[j]) * bit_of(j) for j in range(bits)]

    def span(start, size):
        return pl.ds(pl.multiple_of(start, 8), size)

    def chunk(k):
        return span(k * ch, ch)

    def remote(src, dst, send, recv, where):
        return pltpu.make_async_remote_copy(
            src_ref=src, dst_ref=dst, send_sem=send, recv_sem=recv,
            device_id=where, device_id_type=MESH,
        )

    def loop(low_, high_, body):
        def step(i, carry):
            body(i)
            return carry
        lax.fori_loop(low_, high_, step, 0)

    def lead_copy(k):
        ref = lead.at[chunk(k), :]
        return remote(ref, ref, lead_s.at[k], lead_r.at[k], left)

    def plus_copy(k):
        ref = plus.at[chunk(k), :]
        return remote(ref, ref, plus_s.at[k], plus_r.at[k], right)

    def minus_copy(k):
        ref = minus.at[chunk(k), :]
        return remote(ref, ref, minus_s.at[k], minus_r.at[k], left)

    def own(s, k):
        block = lax.div(r * depth + k * ch, width)
        return scale_ref[s, block] * panel[chunk(k), :]

    def keep(s, k, x):
        high, rest_ = halves(x)
        bh[s, chunk(k), :] = high
        bl[s, chunk(k), :] = rest_

    def plus_step(k):
        @pl.when(c > 0)
        def _():
            plus_copy(k).wait_recv()
            plus[chunk(k), :] = plus[chunk(k), :] + own(1, k)

        @pl.when(c == 0)
        def _():
            plus[chunk(k), :] = own(1, k)

        @pl.when(c < end)
        def _():
            plus_copy(k).start()

    def lead_step(k):
        @pl.when(c < end)
        def _():
            lead_copy(k).wait_recv()

        @pl.when(c == end)
        def _():
            lead[chunk(k), :] = own(0, k)

        @pl.when(c > 0)
        def _():
            lead_copy(k).start()
        keep(0, k, lead[chunk(k), :])

    def minus_step(k):
        @pl.when(c < end - 1)
        def _():
            minus_copy(k).wait_recv()
            minus[chunk(k), :] = minus[chunk(k), :] + own(1, k)

        @pl.when(c == end - 1)
        def _():
            minus[chunk(k), :] = own(1, k)

        @pl.when((c > 0) & (c < end))
        def _():
            minus_copy(k).start()

        @pl.when(c < end)
        def _():
            keep(1, k, (plus[chunk(k), :] + minus[chunk(k), :]) - own(1, k))

        @pl.when(c == end)
        def _():
            keep(1, k, plus[chunk(k), :])

    def quarter_start(q):
        half = (1 - value[0]) + lax.rem(q, 2) * (2 * value[0] - 1)
        return half * (rows // 2) + lax.div(q, 2) * strip

    def a_copy(m):
        k = lax.div(lax.rem(m, n_ch), 4)
        slot = lax.rem(m, ABUF)
        return pltpu.make_async_copy(
            a_ref.at[span(quarter_start(lax.rem(m, 4)), strip),
                     pl.ds(pl.multiple_of(k * kc, 128), kc)],
            abuf.at[slot], a_sem.at[slot],
        )

    tall = min(strip, 512)

    def multiply(m):
        @pl.when(m + ABUF - 1 < 2 * n_ch)
        def _():
            a_copy(m + ABUF - 1).start()

        a_copy(m).wait()
        s = lax.div(m, n_ch)
        k = lax.div(lax.rem(m, n_ch), 4)
        slot = lax.rem(m, ABUF)
        start = quarter_start(lax.rem(m, 4))
        deep = pl.ds(pl.multiple_of(k * kc, 16), kc)

        def body(i):
            a = halves(abuf[slot, span(i * tall, tall), :])
            here = span(start + i * tall, tall)
            part[s, here, :] = part[s, here, :] + dot3(a, (bh[s, deep, :], bl[s, deep, :]))
        loop(0, strip // tall, body)

    def reduce_events(s, h):
        g = 2 * s + h
        src, dst = part.at[s], y.at[s]
        size = [None] + [strip >> j for j in range(bits)]
        start = [None, value[0] * (rows // 2) + h * strip]
        for j in range(1, bits):
            start.append(start[-1] + value[j] * size[j + 1])

        def away(j):
            if j == 0:
                return (1 - value[0]) * (rows // 2) + h * strip
            return start[j] + (1 - value[j]) * size[j + 1]

        def rs(j):
            return remote(src.at[span(away(j), size[j + 1]), :], rs_buf[j].at[g],
                          rs_s.at[g, j], rs_r.at[g, j], {"row": partner[j]})

        def ag(j):
            mine = span(start[1], size[1]) if j == 0 else span(start[j + 1], size[j + 1])
            return remote(dst.at[mine, :], dst.at[mine, :],
                          ag_s.at[g, j], ag_r.at[g, j], {"row": partner[j]})

        def add(j):
            rs(j).wait()
            mine = size[j + 1]
            step = min(mine, 128)

            def body(i):
                here = span(start[j + 1] + i * step, step)
                there = span(i * step, step)
                total = src[here, :] + rs_buf[j][g, there, :]
                if j == bits - 1:
                    block = lax.div(c * rows + start[j + 1] + i * step, width)
                    dst[here, :] = sign_ref[s, block] * total
                else:
                    src[here, :] = total
            loop(0, mine // step, body)

        def event(i):
            if i == 0:
                rs(0).start()
            elif i < bits:
                add(i - 1)
                rs(i).start()
            elif i == bits:
                add(bits - 1)
                ag(bits - 1).start()
            else:
                j = 2 * bits - i
                ag(j).wait()
                if j > 0:
                    ag(j - 1).start()
        return [functools.partial(event, i) for i in range(2 * bits + 1)]

    def share_start(u):
        start = value[0] * (rows // 2) + (u // per) * strip + (u % per) * sub
        for j in range(1, bits):
            start = start + value[j] * (strip >> j)
        return start

    source = lax.div(r * n_cols, n_rows)
    own_start = r * depth - source * rows

    def z_copy(s, u, plane, way, first=False):
        spot = zbuf.at[s, u, plane]
        src = y.at[s, span(share_start(u), sub), :] if first else spot
        sem = zl_s if way < 0 else zr_s
        return remote(src, spot, sem.at[s, u, plane], z_r.at[s, u, plane],
                      left if way < 0 else right)

    def z_own(s, u, way):
        @pl.when((c > 0) if way < 0 else (c < end))
        def _():
            z_copy(s, u, c, way, True).start()

    def target(u, plane):
        at = plane * rows + share_start(u)
        to = lax.div(at, depth)
        return to, at - to * depth

    def give_copy(s, u, plane, to, offset):
        return remote(zbuf.at[s, u, plane], low.at[s, span(offset, sub), :],
                      dl_s.at[s, u, plane], low_r.at[s, lax.div(offset, sub)], {"row": to})

    def z_relay(s, u, d, way):
        plane = c - way * d

        @pl.when((plane >= 0) & (plane <= end))
        def _():
            z_copy(s, u, plane, way).wait_recv()

            @pl.when((c > 0) if way < 0 else (c < end))
            def _():
                z_copy(s, u, plane, way).start()
            to, offset = target(u, plane)

            @pl.when(to == r)
            def _():
                pltpu.make_async_copy(
                    zbuf.at[s, u, plane], low.at[s, span(offset, sub), :],
                    low_r.at[s, lax.div(offset, sub)],
                ).start()

            @pl.when(to != r)
            def _():
                give_copy(s, u, plane, to, offset).start()

    def low_wait(s, i):
        here = low.at[s, span(i * sub, sub), :]
        pltpu.make_async_copy(here, here, low_r.at[s, i]).wait()

    def low_copy(s, i):
        here = span(i * sub, sub)
        return pltpu.make_async_copy(low.at[s, here, :], low_out.at[s, here, :], o_sem.at[s, i])

    def places(u):
        h, k = u // per, u % per
        return [a * (rows // 2) + h * strip + p * piece + k * sub
                for a in range(depth // (rows // 2)) for p in range(strip // piece)]

    def from_y(s, h):
        @pl.when(c == source)
        def _():
            for u in range(h * per, (h + 1) * per):
                for offset in places(u):
                    pltpu.make_async_copy(
                        y.at[s, span(own_start + offset, sub), :],
                        low.at[s, span(offset, sub), :], low_r.at[s, offset // sub],
                    ).start()

    def consume(s, u):
        def one(offset):
            i = lax.div(offset, sub)
            low_wait(s, i)
            here = span(offset, sub)
            low_copy(s, i).start()
            dpart[s] += dot3((bh[s, here, :], bl[s, here, :]), halves(low[s, here, :]),
                             (((0,), (0,)), ((), ())))
        for offset in places(u):
            one(offset)

    ds = width // n_rows

    def other(i):
        return lax.rem(r + i, n_rows)

    def da_copy(s, i, p):
        return remote(dpart.at[s, span(p * ds, ds), :], dbuf.at[s, i],
                      da_s.at[s, p], da_r.at[s, i], {"row": p})

    def db_copy(s, i, p):
        here = dsum.at[s, span(i * ds, ds), :]
        return remote(here, here, db_s.at[s, p], db_r.at[s, i], {"row": p})

    def diag_a(s):
        loop(1, n_rows, lambda i: da_copy(s, r, other(i)).start())

    def diag_b(s):
        mine = span(r * ds, ds)
        dsum[s, mine, :] = dpart[s, mine, :]

        def body(i):
            da_copy(s, other(i), other(i)).wait_recv()
            dsum[s, mine, :] += dbuf[s, other(i)]
        loop(1, n_rows, body)
        loop(1, n_rows, lambda i: db_copy(s, r, other(i)).start())

    def diag_c(s):
        loop(1, n_rows, lambda i: db_copy(s, other(i), other(i)).wait_recv())
        diag_out[s] = dsum[s]

    tb = rows // 8

    def turn_copy(i):
        s, b = i // 8, i % 8
        return pltpu.make_async_copy(
            turned.at[i % 2], y_out.at[s, :, pl.ds(b * tb, tb)], t_sem.at[i % 2]
        )

    def turn(i):
        s, b = i // 8, i % 8
        if i >= 2:
            turn_copy(i - 2).wait()
        turned[i % 2] = y[s, pl.ds(b * tb, tb), :].T
        turn_copy(i).start()

    events = []

    def at(time, f, *args):
        events.append((time, len(events), functools.partial(f, *args)))

    for s in range(2):
        b = n_ch * (s + 1)
        for h in range(2):
            steps = reduce_events(s, h)
            when = [b - 1 + 2 * h, b + 2 + 2 * h]
            when += [b + 7 + 3 * (j - 2) + 3 * h for j in range(2, bits + 1)]
            last = when[bits]
            when += [last + 3 + 4 * j for j in range(bits)]
            for time, f in zip(when, steps):
                at(time, f)
            for u in range(h * per, (h + 1) * per):
                at(last, z_own, s, u, 1)
                at(max(2 * n_ch - 1, last) if s == 0 else last + 6, z_own, s, u, -1)
            at(when[-1], from_y, s, h)
        drift = 2 * n_sub + 1
        for d in range(1, n_cols):
            for u in range(n_sub):
                at(last + 2 + 2 * u + drift * (d - 1), z_relay, s, u, d, 1)
                at(2 * n_ch + 2 + s * (2 * n_sub * end - 1.5) + 2 * u + 2 * n_sub * (d - 1),
                   z_relay, s, u, d, -1)
        final = 2 * n_ch + 2 + (s + 1) * 2 * n_sub * end - 2 * n_sub + 4
        for u in range(n_sub):
            at(final + 2 * u, consume, s, u)
        at(final + 2 * n_sub - 2, diag_a, s)
        at(final + 2 * n_sub + 2, diag_b, s)
        at(final + 2 * n_sub + 6, diag_c, s)
        for i in range(8):
            at(max(2 * n_ch + 14.5, when[-1] + 1) + (1 + s) * i, turn, 8 * s + i)
    events.sort(key=lambda e: e[:2])

    barrier = pltpu.get_barrier_semaphore()
    loop(1, n_rows, lambda i: pl.semaphore_signal(
        barrier, inc=1, device_id={"row": other(i)}, device_id_type=MESH))

    @pl.when(c > 0)
    def _():
        pl.semaphore_signal(barrier, inc=1, device_id=left, device_id_type=MESH)

    @pl.when(c < end)
    def _():
        pl.semaphore_signal(barrier, inc=1, device_id=right, device_id_type=MESH)

    for m in range(ABUF - 1):
        a_copy(m).start()
    dpart[...] = jnp.zeros_like(dpart)

    def clear(i):
        for s in range(2):
            part[s, span(i * strip // 4, strip // 4), :] = jnp.zeros((strip // 4, width), F32)
    loop(0, 16, clear)

    beside = lax.div(c + end - 1, end) + lax.div(2 * end - 1 - c, end)
    pl.semaphore_wait(barrier, n_rows - 1 + beside)

    stop = 2 * n_ch + LAG
    inside = [e for e in events if e[0] < stop]
    outside = [e for e in events if e[0] >= stop]
    times = sorted({e[0] for e in inside})

    def body(u):
        up = u + AHEAD * (end - 2 * c)

        @pl.when((up >= 0) & (up < n_ch))
        def _():
            plus_step(up)

        @pl.when((u >= 0) & (u < n_ch))
        def _():
            lead_step(u)

        @pl.when((u >= n_ch) & (u < 2 * n_ch))
        def _():
            minus_step(u - n_ch)

        @pl.when((u >= LAG) & (u < 2 * n_ch + LAG))
        def _():
            multiply(u - LAG)

        for time in times:
            @pl.when(u == int(time))
            def _(time=time):
                for e in inside:
                    if e[0] == time:
                        e[2]()
    loop(-AHEAD * (end - c), stop, body)
    for e in outside:
        e[2]()

    def drain_panel(k):
        @pl.when(c > 0)
        def _():
            lead_copy(k).wait_send()

        @pl.when((c > 0) & (c < end))
        def _():
            minus_copy(k).wait_send()

        @pl.when(c < end)
        def _():
            plus_copy(k).wait_send()
    loop(0, n_ch, drain_panel)

    for s in range(2):
        for u in range(n_sub):
            def drain(plane, s=s, u=u):
                @pl.when((c > 0) & (plane >= c))
                def _():
                    z_copy(s, u, plane, -1).wait_send()

                @pl.when((c < end) & (plane <= c))
                def _():
                    z_copy(s, u, plane, 1).wait_send()
                to, offset = target(u, plane)

                @pl.when((plane != c) & (to != r))
                def _():
                    give_copy(s, u, plane, to, offset).wait_send()
            loop(0, n_cols, drain)
        loop(1, n_rows, lambda i: da_copy(s, r, other(i)).wait_send())
        loop(1, n_rows, lambda i: db_copy(s, r, other(i)).wait_send())
        loop(0, depth // sub, lambda i: low_copy(s, i).wait())
    turn_copy(14).wait()
    turn_copy(15).wait()


def exchange(n_rows, n_cols, a, panel, scale, sign):
    rows, depth = a.shape
    width = panel.shape[1]
    bits = n_rows.bit_length() - 1
    vmem = pl.BlockSpec(memory_space=pltpu.VMEM)
    smem = pl.BlockSpec(memory_space=pltpu.SMEM)
    anywhere = pl.BlockSpec(memory_space=pl.ANY)
    dma = pltpu.SemaphoreType.DMA
    kc = min(256, depth)
    n = depth // (kc // 4)
    strip = rows // 4
    piece = strip >> (bits - 1)
    sub = min(piece, 128)
    n_sub = 2 * piece // sub
    return pl.pallas_call(
        functools.partial(kernel, n_rows, n_cols),
        out_shape=(
            jax.ShapeDtypeStruct((2, width, rows), F32),
            jax.ShapeDtypeStruct((2, depth, width), F32),
            jax.ShapeDtypeStruct((2, width, width), F32),
        ),
        in_specs=[anywhere, vmem, smem, smem],
        out_specs=(anywhere, anywhere, vmem),
        scratch_shapes=[
            pltpu.VMEM((2, depth, width), BF16),
            pltpu.VMEM((2, depth, width), BF16),
            pltpu.VMEM((depth, width), F32),
            pltpu.VMEM((depth, width), F32),
            pltpu.VMEM((depth, width), F32),
            pltpu.VMEM((2, rows, width), F32),
            pltpu.VMEM((2, rows, width), F32),
            pltpu.VMEM((2, depth, width), F32),
            pltpu.VMEM((2, n_sub, n_cols, sub, width), F32),
            pltpu.VMEM((ABUF, strip, kc), F32),
            pltpu.VMEM((2, width, rows // 8), F32),
            pltpu.VMEM((2, width, width), F32),
            pltpu.VMEM((2, n_rows, width // n_rows, width), F32),
            pltpu.VMEM((2, width, width), F32),
            *[pltpu.VMEM((4, strip >> j, width), F32) for j in range(bits)],
            dma((n,)), dma((n,)), dma((n,)), dma((n,)), dma((n,)), dma((n,)),
            dma((4, bits)), dma((4, bits)), dma((4, bits)), dma((4, bits)),
            dma((2, n_sub, n_cols)), dma((2, n_sub, n_cols)), dma((2, n_sub, n_cols)),
            dma((2, n_sub, n_cols)), dma((2, depth // sub)),
            dma((2, n_rows)), dma((2, n_rows)), dma((2, n_rows)), dma((2, n_rows)),
            dma((ABUF,)), dma((2,)), dma((2, depth // sub)),
        ],
        compiler_params=pltpu.CompilerParams(
            collective_id=0, has_side_effects=True, vmem_limit_bytes=66_000_000
        ),
    )(a, panel, scale, sign)


def settle_kernel(order, y_in, low_in, dsum, dinv, y_out, low_out, diag_out, y_sem, low_sem):
    copies = []
    for s in range(2):
        at = order[s]
        for n, (src, dst, sem) in enumerate([(y_in, y_out, y_sem), (low_in, low_out, low_sem)]):
            parts = sem.shape[1]
            size = src.shape[1] // parts
            for p in range(parts):
                here = pl.ds(p * size, size)
                copies.append(pltpu.make_async_copy(
                    src.at[at, here, :], dst.at[s, here, :], sem.at[s, p]))
    for copy in copies:
        copy.start()
    for s in range(2):
        diag_out[s] = dinv[s] - dsum[order[s]]
    for copy in copies:
        copy.wait()


def settle(order, y, low, dsum, dinv):
    vmem = pl.BlockSpec(memory_space=pltpu.VMEM)
    smem = pl.BlockSpec(memory_space=pltpu.SMEM)
    anywhere = pl.BlockSpec(memory_space=pl.ANY)
    return pl.pallas_call(
        settle_kernel,
        out_shape=tuple(jax.ShapeDtypeStruct(x.shape, F32) for x in (y, low, dinv)),
        in_specs=[smem, anywhere, anywhere, vmem, vmem],
        out_specs=(anywhere, anywhere, vmem),
        scratch_shapes=[pltpu.SemaphoreType.DMA((2, 4)), pltpu.SemaphoreType.DMA((2, 2))],
    )(order, y, low, dsum, dinv)


def shards(inverse_rows, panels, diag_inverse, pattern, owner_slot):
    n_rows, n_cols = lax.axis_size("row"), lax.axis_size("col")
    swap = owner_slot[0] != n_cols - 1
    live = pattern.astype(F32)
    live = jnp.where(swap, live[::-1], live)
    slots = jnp.where(swap, owner_slot[::-1], owner_slot)
    mine = (slots == lax.axis_index("col")).astype(F32)
    first = swap.astype(jnp.int32)
    order = jnp.stack([first, 1 - first])
    y, low, dsum = exchange(
        n_rows, n_cols, inverse_rows, panels[0], live * mine[:, None], -live,
    )
    y, low, diag = settle(order, y, low, dsum, diag_inverse)
    return low, y, diag


def solution(mesh):
    in_specs = (P("col", "row"), P("col", "row", None), P(), P(), P())
    out_specs = (P(None, "row", None), P(None, None, "col"), P())
    return jax.shard_map(shards, mesh=mesh, in_specs=in_specs, out_specs=out_specs, check_vma=False)
```

```python
import functools

import jax
import jax.numpy as jnp
from jax import lax
from jax.experimental import pallas as pl
from jax.experimental.pallas import tpu as pltpu
from jax.sharding import PartitionSpec as P

MESH = pl.DeviceIdType.MESH
F32 = jnp.float32
BF16 = jnp.bfloat16
AHEAD = 4
LAG = 3
ABUF = 4


def halves(x):
    high = x.astype(BF16)
    return high, (x - high.astype(F32)).astype(BF16)


def dot3(a, b, dims=(((1,), (0,)), ((), ()))):
    (ah, al), (bh, bl) = a, b
    dot = functools.partial(lax.dot_general, dimension_numbers=dims, preferred_element_type=F32)
    return dot(ah, bh) + dot(ah, bl) + dot(al, bh)


def kernel(
    n_rows, n_cols,
    a_ref, panel, scale_ref, sign_ref,
    y_out, low_out, diag_out,
    bh, bl, lead, plus, minus, part, y, low, zbuf, abuf, turned, dpart, dbuf, dsum, *rest,
):
    bits = n_rows.bit_length() - 1
    rs_buf = rest[:bits]
    (lead_s, lead_r, plus_s, plus_r, minus_s, minus_r, rs_s, rs_r, ag_s, ag_r,
     zl_s, zr_s, zb_r, zf_s, zg_s, low_r, da_s, da_r, db_s, db_r, a_sem, t_sem, o_sem) = rest[bits:]
    r = lax.axis_index("row")
    c = lax.axis_index("col")
    width = bh.shape[2]
    depth = bh.shape[1]
    rows = y.shape[1]
    end = n_cols - 1
    core = lax.rem(r, 2)
    left, right = {"col": c - 1}, {"col": c + 1}
    strip = rows // 4
    kc = abuf.shape[2]
    ch = kc // 4
    n_ch = depth // ch
    piece = strip >> (bits - 1)
    sub = min(piece, 128)
    per = piece // sub
    n_sub = 2 * per

    def bit_of(j):
        if j == 0:
            return 1
        return (1 << j) + core * ((1 << (bits - j)) - (1 << j))

    value = [lax.rem(lax.div(r, bit_of(j)), 2) for j in range(bits)]
    partner = [r + (1 - 2 * value[j]) * bit_of(j) for j in range(bits)]

    def span(start, size):
        return pl.ds(pl.multiple_of(start, 8), size)

    def chunk(k):
        return span(k * ch, ch)

    def remote(src, dst, send, recv, where):
        return pltpu.make_async_remote_copy(
            src_ref=src, dst_ref=dst, send_sem=send, recv_sem=recv,
            device_id=where, device_id_type=MESH,
        )

    def loop(low_, high_, body):
        def step(i, carry):
            body(i)
            return carry
        lax.fori_loop(low_, high_, step, 0)

    def lead_copy(k):
        ref = lead.at[chunk(k), :]
        return remote(ref, ref, lead_s.at[k], lead_r.at[k], left)

    def plus_copy(k):
        ref = plus.at[chunk(k), :]
        return remote(ref, ref, plus_s.at[k], plus_r.at[k], right)

    def minus_copy(k):
        ref = minus.at[chunk(k), :]
        return remote(ref, ref, minus_s.at[k], minus_r.at[k], left)

    def own(s, k):
        block = lax.div(r * depth + k * ch, width)
        return scale_ref[s, block] * panel[chunk(k), :]

    def keep(s, k, x):
        high, rest_ = halves(x)
        bh[s, chunk(k), :] = high
        bl[s, chunk(k), :] = rest_

    def plus_step(k):
        @pl.when(c > 0)
        def _():
            plus_copy(k).wait_recv()
            plus[chunk(k), :] = plus[chunk(k), :] + own(1, k)

        @pl.when(c == 0)
        def _():
            plus[chunk(k), :] = own(1, k)

        @pl.when(c < end)
        def _():
            plus_copy(k).start()

    def lead_step(k):
        @pl.when(c < end)
        def _():
            lead_copy(k).wait_recv()

        @pl.when(c == end)
        def _():
            lead[chunk(k), :] = own(0, k)

        @pl.when(c > 0)
        def _():
            lead_copy(k).start()
        keep(0, k, lead[chunk(k), :])

    def minus_step(k):
        @pl.when(c < end - 1)
        def _():
            minus_copy(k).wait_recv()
            minus[chunk(k), :] = minus[chunk(k), :] + own(1, k)

        @pl.when(c == end - 1)
        def _():
            minus[chunk(k), :] = own(1, k)

        @pl.when((c > 0) & (c < end))
        def _():
            minus_copy(k).start()

        @pl.when(c < end)
        def _():
            keep(1, k, (plus[chunk(k), :] + minus[chunk(k), :]) - own(1, k))

        @pl.when(c == end)
        def _():
            keep(1, k, plus[chunk(k), :])

    def quarter_start(q):
        half = (1 - value[0]) + lax.rem(q, 2) * (2 * value[0] - 1)
        return half * (rows // 2) + lax.div(q, 2) * strip

    def a_copy(m):
        k = lax.div(lax.rem(m, n_ch), 4)
        slot = lax.rem(m, ABUF)
        return pltpu.make_async_copy(
            a_ref.at[span(quarter_start(lax.rem(m, 4)), strip),
                     pl.ds(pl.multiple_of(k * kc, 128), kc)],
            abuf.at[slot], a_sem.at[slot],
        )

    tall = min(strip, 1024)

    def multiply(m):
        @pl.when(m + ABUF - 1 < 2 * n_ch)
        def _():
            a_copy(m + ABUF - 1).start()

        a_copy(m).wait()
        s = lax.div(m, n_ch)
        k = lax.div(lax.rem(m, n_ch), 4)
        slot = lax.rem(m, ABUF)
        start = quarter_start(lax.rem(m, 4))
        deep = pl.ds(pl.multiple_of(k * kc, 16), kc)

        def body(i):
            a = halves(abuf[slot, span(i * tall, tall), :])
            here = span(start + i * tall, tall)
            part[s, here, :] = part[s, here, :] + dot3(a, (bh[s, deep, :], bl[s, deep, :]))
        loop(0, strip // tall, body)

    def reduce_events(s, h):
        g = 2 * s + h
        src, dst = part.at[s], y.at[s]
        size = [None] + [strip >> j for j in range(bits)]
        start = [None, value[0] * (rows // 2) + h * strip]
        for j in range(1, bits):
            start.append(start[-1] + value[j] * size[j + 1])

        def away(j):
            if j == 0:
                return (1 - value[0]) * (rows // 2) + h * strip
            return start[j] + (1 - value[j]) * size[j + 1]

        def rs(j):
            return remote(src.at[span(away(j), size[j + 1]), :], rs_buf[j].at[g],
                          rs_s.at[g, j], rs_r.at[g, j], {"row": partner[j]})

        def ag(j):
            mine = span(start[1], size[1]) if j == 0 else span(start[j + 1], size[j + 1])
            return remote(dst.at[mine, :], dst.at[mine, :],
                          ag_s.at[g, j], ag_r.at[g, j], {"row": partner[j]})

        def add(j):
            rs(j).wait()
            mine = size[j + 1]
            step = min(mine, 128)

            def body(i):
                here = span(start[j + 1] + i * step, step)
                there = span(i * step, step)
                total = src[here, :] + rs_buf[j][g, there, :]
                if j == bits - 1:
                    block = lax.div(c * rows + start[j + 1] + i * step, width)
                    dst[here, :] = sign_ref[s, block] * total
                else:
                    src[here, :] = total
            loop(0, mine // step, body)

        def cut(copy, i):
            size_ = strip // 8
            here = span(away(0) + i * size_, size_)
            mine = span(start[1] + i * size_, size_)
            if copy is rs:
                remote(src.at[here, :], rs_buf[0].at[g, span(i * size_, size_), :],
                       rs_s.at[g, 0], rs_r.at[g, 0], {"row": partner[0]}).start()
            else:
                remote(dst.at[mine, :], dst.at[mine, :],
                       ag_s.at[g, 0], ag_r.at[g, 0], {"row": partner[0]}).start()

        def event(i):
            if i < bits:
                add(i - 1)
                rs(i).start()
            elif i == bits:
                add(bits - 1)
                ag(bits - 1).start()
            else:
                j = 2 * bits - i
                ag(j).wait()
                if j > 1:
                    ag(j - 1).start()
        return [[functools.partial(cut, f, i) for i in range(8)] for f in (rs, ag)] + [
            functools.partial(event, i) for i in range(1, 2 * bits + 1)]

    def share_start(u):
        start = value[0] * (rows // 2) + (u // per) * strip + (u % per) * sub
        for j in range(1, bits):
            start = start + value[j] * (strip >> j)
        return start

    source = lax.div(r * n_cols, n_rows)
    own_start = r * depth - source * rows

    def target(s, u, plane, to_plane, src, send):
        at = plane * rows + share_start(u)
        to = lax.div(at, depth)
        offset = at - to * depth
        here, recv = low.at[s, span(offset, sub), :], low_r.at[s, lax.div(offset, sub)]
        return to, here, recv, remote(src, here, send, recv, {"row": to, "col": to_plane})

    def share(s, u):
        return y.at[s, span(share_start(u), sub), :]

    def z_copy(s, u, d, way):
        sem = zl_s if way < 0 else zr_s
        return target(s, u, c, c + way * d, share(s, u), sem.at[s, u, d])[3]

    relays = end >= 2

    def relay_copy(s, u):
        return remote(share(s, u), zbuf.at[s, u], zl_s.at[s, u, end], zb_r.at[s, u], {"col": c * 0 + 1})

    def z_all(s, u, way, act):
        if way < 0 and relays:
            @pl.when(c == end)
            def _():
                act(relay_copy(s, u))
        for d in range(end, 0, -1):
            ok = (c >= d) if way < 0 else (c + d <= end)
            if way < 0 and relays:
                ok = ok & ((c < end) | (c - d > 1))

            @pl.when(ok)
            def _(d=d):
                act(z_copy(s, u, d, way))

    def z_send(s, u, way):
        z_all(s, u, way, lambda copy: copy.start())

    def z_relay(s, u):
        @pl.when(c == 1)
        def _():
            relay_copy(s, u).wait_recv()
            src = zbuf.at[s, u]
            target(s, u, end, 0, src, zf_s.at[s, u])[3].start()
            to, here, recv, copy = target(s, u, end, 1, src, zg_s.at[s, u])

            @pl.when(to == r)
            def _():
                pltpu.make_async_copy(src, here, recv).start()

            @pl.when(to != r)
            def _():
                copy.start()

    def z_relay_drain(s, u):
        @pl.when(c == 1)
        def _():
            src = zbuf.at[s, u]
            target(s, u, end, 0, src, zf_s.at[s, u])[3].wait_send()
            to, here, recv, copy = target(s, u, end, 1, src, zg_s.at[s, u])

            @pl.when(to != r)
            def _():
                copy.wait_send()

    def low_wait(s, i):
        here = low.at[s, span(i * sub, sub), :]
        pltpu.make_async_copy(here, here, low_r.at[s, i]).wait()

    def low_copy(s, i):
        here = span(i * sub, sub)
        return pltpu.make_async_copy(low.at[s, here, :], low_out.at[s, here, :], o_sem.at[s, i])

    def places(u):
        h, k = u // per, u % per
        return [a * (rows // 2) + h * strip + p * piece + k * sub
                for a in range(depth // (rows // 2)) for p in range(strip // piece)]

    def from_y(s, h):
        @pl.when(c == source)
        def _():
            for u in range(h * per, (h + 1) * per):
                for offset in places(u):
                    pltpu.make_async_copy(
                        y.at[s, span(own_start + offset, sub), :],
                        low.at[s, span(offset, sub), :], low_r.at[s, offset // sub],
                    ).start()

    def consume(s, u):
        def one(offset):
            i = lax.div(offset, sub)
            low_wait(s, i)
            here = span(offset, sub)
            low_copy(s, i).start()
            dpart[s] += dot3((bh[s, here, :], bl[s, here, :]), halves(low[s, here, :]),
                             (((0,), (0,)), ((), ())))
        for offset in places(u):
            one(offset)

    ds = width // n_rows

    def other(i):
        return lax.rem(r + i, n_rows)

    def da_copy(s, i, p):
        return remote(dpart.at[s, span(p * ds, ds), :], dbuf.at[s, i],
                      da_s.at[s, p], da_r.at[s, i], {"row": p})

    def db_copy(s, i, p):
        here = dsum.at[s, span(i * ds, ds), :]
        return remote(here, here, db_s.at[s, p], db_r.at[s, i], {"row": p})

    def diag_a(s):
        loop(1, n_rows, lambda i: da_copy(s, r, other(i)).start())

    def diag_b(s):
        mine = span(r * ds, ds)
        dsum[s, mine, :] = dpart[s, mine, :]

        def body(i):
            da_copy(s, other(i), other(i)).wait_recv()
            dsum[s, mine, :] += dbuf[s, other(i)]
        loop(1, n_rows, body)
        loop(1, n_rows, lambda i: db_copy(s, r, other(i)).start())

    def diag_c(s):
        loop(1, n_rows, lambda i: db_copy(s, other(i), other(i)).wait_recv())
        diag_out[s] = dsum[s]

    tb = rows // 8

    def turn_copy(i):
        s, b = i // 8, i % 8
        return pltpu.make_async_copy(
            turned.at[i % 2], y_out.at[s, :, pl.ds(b * tb, tb)], t_sem.at[i % 2]
        )

    def turn(i):
        s, b = i // 8, i % 8
        if i >= 2:
            turn_copy(i - 2).wait()
        turned[i % 2] = y[s, pl.ds(b * tb, tb), :].T
        turn_copy(i).start()

    events = []

    def at(time, f, *args):
        events.append((time, len(events), functools.partial(f, *args)))

    full = 2 * n_ch
    for s in range(2):
        b = n_ch * (s + 1)
        for h in range(2):
            out, back, *steps = reduce_events(s, h)
            when = [b + 5 + 4 * h] if s == 0 else [b + 4 + 2 * h]
            when += [b + 11 + 5 * (j - 2) + 4 * h for j in range(2, bits + 1)]
            last = when[-1]
            when += [last + 5 + 6 * j for j in range(bits)]
            for n, f in enumerate(out):
                at(b - 1 + 4 * h + n // 2 if s == 0 else b - 1 + 2 * h, f)
            for n, f in enumerate(back):
                at(when[-2] + (n // 2 if s == 0 else 0) + 0.25, f)
            for time, f in zip(when, steps):
                at(time, f)
            for u in range(h * per, (h + 1) * per):
                at(max(full - 2, last), z_send, s, u, 1)
                at(max(full - 1, last), z_send, s, u, -1)
            at(when[-1], from_y, s, h)
        done = when[-1]
        if relays:
            for u in range(n_sub):
                at(full + 21.5 + u if s == 0 else full + 40.5 + 2 * u, z_relay, s, u)
        for i in range(8):
            at(max(full + (20.5 if s == 0 else 39.5), done + 0.5) + i, turn, 8 * s + i)
        final = full + (35 if s == 0 else 50)
        for u in range(n_sub):
            at(final + u, consume, s, u)
        at(final + n_sub, diag_a, s)
        at(final + n_sub + (8 if s == 0 else 1), diag_b, s)
        at(final + n_sub + (10 if s == 0 else 2), diag_c, s)
    events.sort(key=lambda e: e[:2])

    barrier = pltpu.get_barrier_semaphore()
    loop(1, n_rows, lambda i: pl.semaphore_signal(
        barrier, inc=1, device_id={"row": other(i)}, device_id_type=MESH))

    @pl.when(c > 0)
    def _():
        pl.semaphore_signal(barrier, inc=1, device_id=left, device_id_type=MESH)

    @pl.when(c < end)
    def _():
        pl.semaphore_signal(barrier, inc=1, device_id=right, device_id_type=MESH)

    for m in range(ABUF - 1):
        a_copy(m).start()
    dpart[...] = jnp.zeros_like(dpart)

    def clear(i):
        for s in range(2):
            part[s, span(i * strip // 4, strip // 4), :] = jnp.zeros((strip // 4, width), F32)
    loop(0, 16, clear)

    beside = lax.div(c + end - 1, end) + lax.div(2 * end - 1 - c, end)
    pl.semaphore_wait(barrier, n_rows - 1 + beside)

    stop = 2 * n_ch + LAG
    inside = [e for e in events if e[0] < stop]
    outside = [e for e in events if e[0] >= stop]
    times = sorted({e[0] for e in inside})

    def body(u):
        up = u + AHEAD * (end - 2 * c)

        @pl.when((up >= 0) & (up < n_ch))
        def _():
            plus_step(up)

        @pl.when((u >= 0) & (u < n_ch))
        def _():
            lead_step(u)

        @pl.when((u >= n_ch) & (u < 2 * n_ch))
        def _():
            minus_step(u - n_ch)

        @pl.when((u >= LAG) & (u < 2 * n_ch + LAG))
        def _():
            multiply(u - LAG)

        for time in times:
            @pl.when(u == int(time))
            def _(time=time):
                for e in inside:
                    if e[0] == time:
                        e[2]()
    loop(-AHEAD * (end - c), stop, body)
    for e in outside:
        e[2]()

    def drain_panel(k):
        @pl.when(c > 0)
        def _():
            lead_copy(k).wait_send()

        @pl.when((c > 0) & (c < end))
        def _():
            minus_copy(k).wait_send()

        @pl.when(c < end)
        def _():
            plus_copy(k).wait_send()
    loop(0, n_ch, drain_panel)

    for s in range(2):
        for u in range(n_sub):
            for way in (-1, 1):
                z_all(s, u, way, lambda copy: copy.wait_send())
            if relays:
                z_relay_drain(s, u)
        loop(1, n_rows, lambda i: da_copy(s, r, other(i)).wait_send())
        loop(1, n_rows, lambda i: db_copy(s, r, other(i)).wait_send())
        loop(0, depth // sub, lambda i: low_copy(s, i).wait())
    turn_copy(14).wait()
    turn_copy(15).wait()


def exchange(n_rows, n_cols, a, panel, scale, sign):
    rows, depth = a.shape
    width = panel.shape[1]
    bits = n_rows.bit_length() - 1
    vmem = pl.BlockSpec(memory_space=pltpu.VMEM)
    smem = pl.BlockSpec(memory_space=pltpu.SMEM)
    anywhere = pl.BlockSpec(memory_space=pl.ANY)
    dma = pltpu.SemaphoreType.DMA
    kc = min(256, depth)
    n = depth // (kc // 4)
    strip = rows // 4
    piece = strip >> (bits - 1)
    sub = min(piece, 128)
    n_sub = 2 * piece // sub
    return pl.pallas_call(
        functools.partial(kernel, n_rows, n_cols),
        out_shape=(
            jax.ShapeDtypeStruct((2, width, rows), F32),
            jax.ShapeDtypeStruct((2, depth, width), F32),
            jax.ShapeDtypeStruct((2, width, width), F32),
        ),
        in_specs=[anywhere, vmem, smem, smem],
        out_specs=(anywhere, anywhere, vmem),
        scratch_shapes=[
            pltpu.VMEM((2, depth, width), BF16),
            pltpu.VMEM((2, depth, width), BF16),
            pltpu.VMEM((depth, width), F32),
            pltpu.VMEM((depth, width), F32),
            pltpu.VMEM((depth, width), F32),
            pltpu.VMEM((2, rows, width), F32),
            pltpu.VMEM((2, rows, width), F32),
            pltpu.VMEM((2, depth, width), F32),
            pltpu.VMEM((2, n_sub, sub, width), F32),
            pltpu.VMEM((ABUF, strip, kc), F32),
            pltpu.VMEM((2, width, rows // 8), F32),
            pltpu.VMEM((2, width, width), F32),
            pltpu.VMEM((2, n_rows, width // n_rows, width), F32),
            pltpu.VMEM((2, width, width), F32),
            *[pltpu.VMEM((4, strip >> j, width), F32) for j in range(bits)],
            dma((n,)), dma((n,)), dma((n,)), dma((n,)), dma((n,)), dma((n,)),
            dma((4, bits)), dma((4, bits)), dma((4, bits)), dma((4, bits)),
            dma((2, n_sub, n_cols)), dma((2, n_sub, n_cols)),
            dma((2, n_sub)), dma((2, n_sub)), dma((2, n_sub)), dma((2, depth // sub)),
            dma((2, n_rows)), dma((2, n_rows)), dma((2, n_rows)), dma((2, n_rows)),
            dma((ABUF,)), dma((2,)), dma((2, depth // sub)),
        ],
        compiler_params=pltpu.CompilerParams(
            collective_id=0, has_side_effects=True, vmem_limit_bytes=66_000_000
        ),
    )(a, panel, scale, sign)


def settle_kernel(order, y_in, low_in, dsum, dinv, y_out, low_out, diag_out):
    y_out[...] = y_in[...]
    low_out[...] = low_in[...]
    diag_out[...] = dinv[...] - dsum[...]


def settle(order, y, low, dsum, dinv):
    parts = 4

    def spec(x, moved):
        block = (1, x.shape[1] // parts, x.shape[2])
        if moved:
            return pl.BlockSpec(block, lambda s, p, order: (order[s], p, 0))
        return pl.BlockSpec(block, lambda s, p, order: (s, p, 0))
    outs = (y, low, dinv)
    return pl.pallas_call(
        settle_kernel,
        out_shape=tuple(jax.ShapeDtypeStruct(x.shape, F32) for x in outs),
        grid_spec=pltpu.PrefetchScalarGridSpec(
            num_scalar_prefetch=1, grid=(2, parts),
            in_specs=[spec(y, True), spec(low, True), spec(dsum, True), spec(dinv, False)],
            out_specs=tuple(spec(x, False) for x in outs),
        ),
    )(order, y, low, dsum, dinv)


def shards(inverse_rows, panels, diag_inverse, pattern, owner_slot):
    n_rows, n_cols = lax.axis_size("row"), lax.axis_size("col")
    swap = owner_slot[0] != n_cols - 1
    live = pattern.astype(F32)
    live = jnp.where(swap, live[::-1], live)
    slots = jnp.where(swap, owner_slot[::-1], owner_slot)
    mine = (slots == lax.axis_index("col")).astype(F32)
    first = swap.astype(jnp.int32)
    order = jnp.stack([first, 1 - first])
    y, low, dsum = exchange(
        n_rows, n_cols, inverse_rows, panels[0], live * mine[:, None], -live,
    )
    y, low, diag = settle(order, y, low, dsum, diag_inverse)
    return low, y, diag


def solution(mesh):
    in_specs = (P("col", "row"), P("col", "row", None), P(), P(), P())
    out_specs = (P(None, "row", None), P(None, None, "col"), P())
    return jax.shard_map(shards, mesh=mesh, in_specs=in_specs, out_specs=out_specs, check_vma=False)
```

```python
import functools

import jax
import jax.numpy as jnp
from jax import lax
from jax.experimental import pallas as pl
from jax.experimental.pallas import tpu as pltpu
from jax.sharding import PartitionSpec as P

MESH = pl.DeviceIdType.MESH
F32 = jnp.float32
BF16 = jnp.bfloat16
AHEAD = 4
LAG = 3
ABUF = 4


def halves(x):
    high = x.astype(BF16)
    return high, (x - high.astype(F32)).astype(BF16)


def dot3(a, b, dims=(((1,), (0,)), ((), ()))):
    (ah, al), (bh, bl) = a, b
    dot = functools.partial(lax.dot_general, dimension_numbers=dims, preferred_element_type=F32)
    return dot(ah, bh) + dot(ah, bl) + dot(al, bh)


def kernel(
    n_rows, n_cols,
    a_ref, panel, pattern_ref, slot_ref,
    y_out, low_out, diag_out,
    bh, bl, lead, plus, minus, part, y, low, zbuf, abuf, turned, dpart, dbuf, dsum, *rest,
):
    bits = n_rows.bit_length() - 1
    rs_buf = rest[:bits]
    (lead_s, lead_r, plus_s, plus_r, minus_s, minus_r, rs_s, rs_r, ag_s, ag_r,
     zl_s, zr_s, zb_r, zf_s, zg_s, low_r, da_s, da_r, db_s, db_r, a_sem, t_sem, o_sem) = rest[bits:]
    r = lax.axis_index("row")
    c = lax.axis_index("col")
    width = bh.shape[2]
    depth = bh.shape[1]
    rows = y.shape[1]
    end = n_cols - 1
    core = lax.rem(r, 2)
    left, right = {"col": c - 1}, {"col": c + 1}
    strip = rows // 4
    kc = abuf.shape[2]
    ch = kc // 4
    n_ch = depth // ch
    piece = strip >> (bits - 1)
    sub = min(piece, 128)
    per = piece // sub
    n_sub = 2 * per

    def bit_of(j):
        if j == 0:
            return 1
        return (1 << j) + core * ((1 << (bits - j)) - (1 << j))

    value = [lax.rem(lax.div(r, bit_of(j)), 2) for j in range(bits)]
    partner = [r + (1 - 2 * value[j]) * bit_of(j) for j in range(bits)]

    def span(start, size):
        return pl.ds(pl.multiple_of(start, 8), size)

    def chunk(k):
        return span(k * ch, ch)

    def remote(src, dst, send, recv, where):
        return pltpu.make_async_remote_copy(
            src_ref=src, dst_ref=dst, send_sem=send, recv_sem=recv,
            device_id=where, device_id_type=MESH,
        )

    def loop(low_, high_, body):
        def step(i, carry):
            body(i)
            return carry
        lax.fori_loop(low_, high_, step, 0)

    def lead_copy(k):
        ref = lead.at[chunk(k), :]
        return remote(ref, ref, lead_s.at[k], lead_r.at[k], left)

    def plus_copy(k):
        ref = plus.at[chunk(k), :]
        return remote(ref, ref, plus_s.at[k], plus_r.at[k], right)

    def minus_copy(k):
        ref = minus.at[chunk(k), :]
        return remote(ref, ref, minus_s.at[k], minus_r.at[k], left)

    lead_at = jnp.where(slot_ref[0] == end, 0, 1)

    def live(s, block):
        at_ = lead_at if s == 0 else 1 - lead_at
        return pattern_ref[at_, block].astype(F32)

    def own(s, k):
        block = lax.div(r * depth + k * ch, width)
        at_ = lead_at if s == 0 else 1 - lead_at
        here = jnp.where(slot_ref[at_] == c, 1.0, 0.0)
        return (live(s, block) * here) * panel[chunk(k), :]

    def keep(s, k, x):
        high, rest_ = halves(x)
        bh[s, chunk(k), :] = high
        bl[s, chunk(k), :] = rest_

    def plus_step(k):
        @pl.when(c > 0)
        def _():
            plus_copy(k).wait_recv()
            plus[chunk(k), :] = plus[chunk(k), :] + own(1, k)

        @pl.when(c == 0)
        def _():
            plus[chunk(k), :] = own(1, k)

        @pl.when(c < end)
        def _():
            plus_copy(k).start()

    def lead_step(k):
        @pl.when(c < end)
        def _():
            lead_copy(k).wait_recv()

        @pl.when(c == end)
        def _():
            lead[chunk(k), :] = own(0, k)

        @pl.when(c > 0)
        def _():
            lead_copy(k).start()
        keep(0, k, lead[chunk(k), :])

    def minus_step(k):
        @pl.when(c < end - 1)
        def _():
            minus_copy(k).wait_recv()
            minus[chunk(k), :] = minus[chunk(k), :] + own(1, k)

        @pl.when(c == end - 1)
        def _():
            minus[chunk(k), :] = own(1, k)

        @pl.when((c > 0) & (c < end))
        def _():
            minus_copy(k).start()

        @pl.when(c < end)
        def _():
            keep(1, k, (plus[chunk(k), :] + minus[chunk(k), :]) - own(1, k))

        @pl.when(c == end)
        def _():
            keep(1, k, plus[chunk(k), :])

    def quarter_start(q):
        half = (1 - value[0]) + lax.rem(q, 2) * (2 * value[0] - 1)
        return half * (rows // 2) + lax.div(q, 2) * strip

    def a_copy(m):
        k = lax.div(lax.rem(m, n_ch), 4)
        slot = lax.rem(m, ABUF)
        return pltpu.make_async_copy(
            a_ref.at[span(quarter_start(lax.rem(m, 4)), strip),
                     pl.ds(pl.multiple_of(k * kc, 128), kc)],
            abuf.at[slot], a_sem.at[slot],
        )

    tall = min(strip, 1024)

    def multiply(m):
        @pl.when(m + ABUF - 1 < 2 * n_ch)
        def _():
            a_copy(m + ABUF - 1).start()

        a_copy(m).wait()
        s = lax.div(m, n_ch)
        k = lax.div(lax.rem(m, n_ch), 4)
        slot = lax.rem(m, ABUF)
        start = quarter_start(lax.rem(m, 4))
        deep = pl.ds(pl.multiple_of(k * kc, 16), kc)

        def body(i):
            a = halves(abuf[slot, span(i * tall, tall), :])
            here = span(start + i * tall, tall)
            part[s, here, :] = part[s, here, :] + dot3(a, (bh[s, deep, :], bl[s, deep, :]))
        loop(0, strip // tall, body)

    def reduce_events(s, h):
        g = 2 * s + h
        src, dst = part.at[s], y.at[s]
        size = [None] + [strip >> j for j in range(bits)]
        start = [None, value[0] * (rows // 2) + h * strip]
        for j in range(1, bits):
            start.append(start[-1] + value[j] * size[j + 1])

        def away(j):
            if j == 0:
                return (1 - value[0]) * (rows // 2) + h * strip
            return start[j] + (1 - value[j]) * size[j + 1]

        def rs(j):
            return remote(src.at[span(away(j), size[j + 1]), :], rs_buf[j].at[g],
                          rs_s.at[g, j], rs_r.at[g, j], {"row": partner[j]})

        def ag(j):
            mine = span(start[1], size[1]) if j == 0 else span(start[j + 1], size[j + 1])
            return remote(dst.at[mine, :], dst.at[mine, :],
                          ag_s.at[g, j], ag_r.at[g, j], {"row": partner[j]})

        def add(j):
            rs(j).wait()
            mine = size[j + 1]
            step = min(mine, 128)

            def body(i):
                here = span(start[j + 1] + i * step, step)
                there = span(i * step, step)
                total = src[here, :] + rs_buf[j][g, there, :]
                if j == bits - 1:
                    block = lax.div(c * rows + start[j + 1] + i * step, width)
                    dst[here, :] = -live(s, block) * total
                else:
                    src[here, :] = total
            loop(0, mine // step, body)

        def cut(copy, i):
            size_ = strip // 8
            here = span(away(0) + i * size_, size_)
            mine = span(start[1] + i * size_, size_)
            if copy is rs:
                remote(src.at[here, :], rs_buf[0].at[g, span(i * size_, size_), :],
                       rs_s.at[g, 0], rs_r.at[g, 0], {"row": partner[0]}).start()
            else:
                remote(dst.at[mine, :], dst.at[mine, :],
                       ag_s.at[g, 0], ag_r.at[g, 0], {"row": partner[0]}).start()

        def event(i):
            if i < bits:
                add(i - 1)
                rs(i).start()
            elif i == bits:
                add(bits - 1)
                ag(bits - 1).start()
            else:
                j = 2 * bits - i
                ag(j).wait()
                if j > 1:
                    ag(j - 1).start()
        return [[functools.partial(cut, f, i) for i in range(8)] for f in (rs, ag)] + [
            functools.partial(event, i) for i in range(1, 2 * bits + 1)]

    def share_start(u):
        start = value[0] * (rows // 2) + (u // per) * strip + (u % per) * sub
        for j in range(1, bits):
            start = start + value[j] * (strip >> j)
        return start

    source = lax.div(r * n_cols, n_rows)
    own_start = r * depth - source * rows

    def target(s, u, plane, to_plane, src, send):
        at = plane * rows + share_start(u)
        to = lax.div(at, depth)
        offset = at - to * depth
        here, recv = low.at[s, span(offset, sub), :], low_r.at[s, lax.div(offset, sub)]
        return to, here, recv, remote(src, here, send, recv, {"row": to, "col": to_plane})

    def share(s, u):
        return y.at[s, span(share_start(u), sub), :]

    def z_copy(s, u, d, way):
        sem = zl_s if way < 0 else zr_s
        return target(s, u, c, c + way * d, share(s, u), sem.at[s, u, d])[3]

    relays = end >= 2

    def relay_copy(s, u):
        return remote(share(s, u), zbuf.at[s, u], zl_s.at[s, u, end], zb_r.at[s, u], {"col": c * 0 + 1})

    def z_all(s, u, way, act):
        if way < 0 and relays:
            @pl.when(c == end)
            def _():
                act(relay_copy(s, u))
        for d in range(end, 0, -1):
            ok = (c >= d) if way < 0 else (c + d <= end)
            if way < 0 and relays:
                ok = ok & ((c < end) | (c - d > 1))

            @pl.when(ok)
            def _(d=d):
                act(z_copy(s, u, d, way))

    def z_send(s, u, way):
        z_all(s, u, way, lambda copy: copy.start())

    def z_relay(s, u):
        @pl.when(c == 1)
        def _():
            relay_copy(s, u).wait_recv()
            src = zbuf.at[s, u]
            target(s, u, end, 0, src, zf_s.at[s, u])[3].start()
            to, here, recv, copy = target(s, u, end, 1, src, zg_s.at[s, u])

            @pl.when(to == r)
            def _():
                pltpu.make_async_copy(src, here, recv).start()

            @pl.when(to != r)
            def _():
                copy.start()

    def z_relay_drain(s, u):
        @pl.when(c == 1)
        def _():
            src = zbuf.at[s, u]
            target(s, u, end, 0, src, zf_s.at[s, u])[3].wait_send()
            to, here, recv, copy = target(s, u, end, 1, src, zg_s.at[s, u])

            @pl.when(to != r)
            def _():
                copy.wait_send()

    def low_wait(s, i):
        here = low.at[s, span(i * sub, sub), :]
        pltpu.make_async_copy(here, here, low_r.at[s, i]).wait()

    def low_copy(s, i):
        here = span(i * sub, sub)
        return pltpu.make_async_copy(low.at[s, here, :], low_out.at[s, here, :], o_sem.at[s, i])

    def places(u):
        h, k = u // per, u % per
        return [a * (rows // 2) + h * strip + p * piece + k * sub
                for a in range(depth // (rows // 2)) for p in range(strip // piece)]

    def from_y(s, h):
        @pl.when(c == source)
        def _():
            for u in range(h * per, (h + 1) * per):
                for offset in places(u):
                    pltpu.make_async_copy(
                        y.at[s, span(own_start + offset, sub), :],
                        low.at[s, span(offset, sub), :], low_r.at[s, offset // sub],
                    ).start()

    def consume(s, u):
        def one(offset):
            i = lax.div(offset, sub)
            low_wait(s, i)
            here = span(offset, sub)
            low_copy(s, i).start()
            dpart[s] += dot3((bh[s, here, :], bl[s, here, :]), halves(low[s, here, :]),
                             (((0,), (0,)), ((), ())))
        for offset in places(u):
            one(offset)

    ds = width // n_rows

    def other(i):
        return lax.rem(r + i, n_rows)

    def da_copy(s, i, p):
        return remote(dpart.at[s, span(p * ds, ds), :], dbuf.at[s, i],
                      da_s.at[s, p], da_r.at[s, i], {"row": p})

    def db_copy(s, i, p):
        here = dsum.at[s, span(i * ds, ds), :]
        return remote(here, here, db_s.at[s, p], db_r.at[s, i], {"row": p})

    def diag_a(s):
        loop(1, n_rows, lambda i: da_copy(s, r, other(i)).start())

    def diag_b(s):
        mine = span(r * ds, ds)
        dsum[s, mine, :] = dpart[s, mine, :]

        def body(i):
            da_copy(s, other(i), other(i)).wait_recv()
            dsum[s, mine, :] += dbuf[s, other(i)]
        loop(1, n_rows, body)
        loop(1, n_rows, lambda i: db_copy(s, r, other(i)).start())

    def diag_c(s):
        loop(1, n_rows, lambda i: db_copy(s, other(i), other(i)).wait_recv())
        diag_out[s] = dsum[s]

    tb = rows // 8

    def turn_copy(i):
        s, b = i // 8, i % 8
        return pltpu.make_async_copy(
            turned.at[b], y_out.at[s, :, pl.ds(b * tb, tb)], t_sem.at[b]
        )

    def turn(i):
        s, b = i // 8, i % 8
        if s > 0:
            turn_copy(i - 8).wait()
        turned[b] = y[s, pl.ds(b * tb, tb), :].T
        turn_copy(i).start()

    events = []

    def at(time, f, *args):
        events.append((time, len(events), functools.partial(f, *args)))

    full = 2 * n_ch
    for s in range(2):
        b = n_ch * (s + 1)
        for h in range(2):
            out, back, *steps = reduce_events(s, h)
            when = [b + 5 + 4 * h] if s == 0 else [b + 4 + 2 * h]
            when += [b + 11 + 5 * (j - 2) + 4 * h for j in range(2, bits + 1)]
            last = when[-1]
            when += [last + 5 + 6 * j for j in range(bits)]
            for n, f in enumerate(out):
                at(b - 1 + 4 * h + n // 2 if s == 0 else b - 1 + 2 * h, f)
            for n, f in enumerate(back):
                at(when[-2] + (n // 2 if s == 0 else 0) + 0.25, f)
            for time, f in zip(when, steps):
                at(time, f)
            for u in range(h * per, (h + 1) * per):
                at(max(full - 2, last), z_send, s, u, 1)
                at(max(full - 1, last), z_send, s, u, -1)
            at(when[-1], from_y, s, h)
        done = when[-1]
        if relays:
            for u in range(n_sub):
                at(full + (21.5 + u if s == 0 else 31.5 + u / n_sub), z_relay, s, u)
        for i in range(8):
            at(max(full + (25.5 if s == 0 else 0), done + 0.5) + i / 8, turn, 8 * s + i)
        final = full + (28 if s == 0 else 50)
        for u in range(n_sub):
            at(final + u / n_sub, consume, s, u)
        at(final + 1, diag_a, s)
        at(full + (49 if s == 0 else 52), diag_b, s)
        at(full + 53, diag_c, s)
    events.sort(key=lambda e: e[:2])

    barrier = pltpu.get_barrier_semaphore()
    loop(1, n_rows, lambda i: pl.semaphore_signal(
        barrier, inc=1, device_id={"row": other(i)}, device_id_type=MESH))

    @pl.when(c > 0)
    def _():
        pl.semaphore_signal(barrier, inc=1, device_id=left, device_id_type=MESH)

    @pl.when(c < end)
    def _():
        pl.semaphore_signal(barrier, inc=1, device_id=right, device_id_type=MESH)

    for m in range(ABUF - 1):
        a_copy(m).start()
    dpart[...] = jnp.zeros_like(dpart)

    def clear(i):
        for s in range(2):
            part[s, span(i * strip // 4, strip // 4), :] = jnp.zeros((strip // 4, width), F32)
    loop(0, 16, clear)

    beside = lax.div(c + end - 1, end) + lax.div(2 * end - 1 - c, end)
    pl.semaphore_wait(barrier, n_rows - 1 + beside)

    stop = 2 * n_ch + LAG
    inside = [e for e in events if e[0] < stop]
    outside = [e for e in events if e[0] >= stop]
    times = sorted({e[0] for e in inside})

    def body(u):
        up = u + AHEAD * (end - 2 * c)

        @pl.when((up >= 0) & (up < n_ch))
        def _():
            plus_step(up)

        @pl.when((u >= 0) & (u < n_ch))
        def _():
            lead_step(u)

        @pl.when((u >= n_ch) & (u < 2 * n_ch))
        def _():
            minus_step(u - n_ch)

        @pl.when((u >= LAG) & (u < 2 * n_ch + LAG))
        def _():
            multiply(u - LAG)

        for time in times:
            @pl.when(u == int(time))
            def _(time=time):
                for e in inside:
                    if e[0] == time:
                        e[2]()
    loop(-AHEAD * (end - c), stop, body)
    for e in outside:
        e[2]()

    def drain_panel(k):
        @pl.when(c > 0)
        def _():
            lead_copy(k).wait_send()

        @pl.when((c > 0) & (c < end))
        def _():
            minus_copy(k).wait_send()

        @pl.when(c < end)
        def _():
            plus_copy(k).wait_send()
    loop(0, n_ch, drain_panel)

    for s in range(2):
        for u in range(n_sub):
            for way in (-1, 1):
                z_all(s, u, way, lambda copy: copy.wait_send())
            if relays:
                z_relay_drain(s, u)
        loop(1, n_rows, lambda i: da_copy(s, r, other(i)).wait_send())
        loop(1, n_rows, lambda i: db_copy(s, r, other(i)).wait_send())
        loop(0, depth // sub, lambda i: low_copy(s, i).wait())
    for i in range(8, 16):
        turn_copy(i).wait()


def exchange(n_rows, n_cols, a, panel, pattern, slots):
    rows, depth = a.shape
    width = panel.shape[1]
    bits = n_rows.bit_length() - 1
    vmem = pl.BlockSpec(memory_space=pltpu.VMEM)
    smem = pl.BlockSpec(memory_space=pltpu.SMEM)
    anywhere = pl.BlockSpec(memory_space=pl.ANY)
    dma = pltpu.SemaphoreType.DMA
    kc = min(256, depth)
    n = depth // (kc // 4)
    strip = rows // 4
    piece = strip >> (bits - 1)
    sub = min(piece, 128)
    n_sub = 2 * piece // sub
    return pl.pallas_call(
        functools.partial(kernel, n_rows, n_cols),
        out_shape=(
            jax.ShapeDtypeStruct((2, width, rows), F32),
            jax.ShapeDtypeStruct((2, depth, width), F32),
            jax.ShapeDtypeStruct((2, width, width), F32),
        ),
        in_specs=[anywhere, vmem, smem, smem],
        out_specs=(anywhere, anywhere, vmem),
        scratch_shapes=[
            pltpu.VMEM((2, depth, width), BF16),
            pltpu.VMEM((2, depth, width), BF16),
            pltpu.VMEM((depth, width), F32),
            pltpu.VMEM((depth, width), F32),
            pltpu.VMEM((depth, width), F32),
            pltpu.VMEM((2, rows, width), F32),
            pltpu.VMEM((2, rows, width), F32),
            pltpu.VMEM((2, depth, width), F32),
            pltpu.VMEM((2, n_sub, sub, width), F32),
            pltpu.VMEM((ABUF, strip, kc), F32),
            pltpu.VMEM((8, width, rows // 8), F32),
            pltpu.VMEM((2, width, width), F32),
            pltpu.VMEM((2, n_rows, width // n_rows, width), F32),
            pltpu.VMEM((2, width, width), F32),
            *[pltpu.VMEM((4, strip >> j, width), F32) for j in range(bits)],
            dma((n,)), dma((n,)), dma((n,)), dma((n,)), dma((n,)), dma((n,)),
            dma((4, bits)), dma((4, bits)), dma((4, bits)), dma((4, bits)),
            dma((2, n_sub, n_cols)), dma((2, n_sub, n_cols)),
            dma((2, n_sub)), dma((2, n_sub)), dma((2, n_sub)), dma((2, depth // sub)),
            dma((2, n_rows)), dma((2, n_rows)), dma((2, n_rows)), dma((2, n_rows)),
            dma((ABUF,)), dma((8,)), dma((2, depth // sub)),
        ],
        compiler_params=pltpu.CompilerParams(
            collective_id=0, has_side_effects=True, vmem_limit_bytes=66_000_000
        ),
    )(a, panel, pattern, slots)


def settle_kernel(slots, y_in, low_in, dsum, dinv, y_out, low_out, diag_out):
    y_out[...] = y_in[...]
    low_out[...] = low_in[...]
    diag_out[...] = dinv[...] - dsum[...]


def settle(n_cols, slots, y, low, dsum, dinv):
    parts = 4

    def spec(x, moved):
        block = (1, x.shape[1] // parts, x.shape[2])
        if moved:
            return pl.BlockSpec(block, lambda s, p, slots: (
                jnp.where(slots[0] == n_cols - 1, s, 1 - s), p, 0))
        return pl.BlockSpec(block, lambda s, p, slots: (s, p, 0))
    outs = (y, low, dinv)
    return pl.pallas_call(
        settle_kernel,
        out_shape=tuple(jax.ShapeDtypeStruct(x.shape, F32) for x in outs),
        grid_spec=pltpu.PrefetchScalarGridSpec(
            num_scalar_prefetch=1, grid=(2, parts),
            in_specs=[spec(y, True), spec(low, True), spec(dsum, True), spec(dinv, False)],
            out_specs=tuple(spec(x, False) for x in outs),
        ),
    )(slots, y, low, dsum, dinv)


def shards(inverse_rows, panels, diag_inverse, pattern, owner_slot):
    n_rows, n_cols = lax.axis_size("row"), lax.axis_size("col")
    y, low, dsum = exchange(n_rows, n_cols, inverse_rows, panels[0], pattern, owner_slot)
    y, low, diag = settle(n_cols, owner_slot, y, low, dsum, diag_inverse)
    return low, y, diag


def solution(mesh):
    in_specs = (P("col", "row"), P("col", "row", None), P(), P(), P())
    out_specs = (P(None, "row", None), P(None, None, "col"), P())
    return jax.shard_map(shards, mesh=mesh, in_specs=in_specs, out_specs=out_specs, check_vma=False)
```

```python
import functools

import jax
import jax.numpy as jnp
from jax import lax
from jax.experimental import pallas as pl
from jax.experimental.pallas import tpu as pltpu
from jax.sharding import PartitionSpec as P

MESH = pl.DeviceIdType.MESH
F32 = jnp.float32
BF16 = jnp.bfloat16
AHEAD = 3
LAG = 3
ABUF = 4


def halves(x):
    high = x.astype(BF16)
    return high, (x - high.astype(F32)).astype(BF16)


def dot3(a, b, dims=(((1,), (0,)), ((), ()))):
    (ah, al), (bh, bl) = a, b
    dot = functools.partial(lax.dot_general, dimension_numbers=dims, preferred_element_type=F32)
    return dot(ah, bh) + dot(ah, bl) + dot(al, bh)


def kernel(
    n_rows, n_cols,
    a_ref, panel, pattern_ref, slot_ref,
    y_out, low_out, diag_out,
    bh, bl, lead, plus, minus, part, y, low, abuf, turned, dpart, dbuf, dsum, *rest,
):
    bits = n_rows.bit_length() - 1
    rs_buf = rest[:bits]
    (lead_s, lead_r, plus_s, plus_r, minus_s, minus_r, rs_s, rs_r, ag_s, ag_r,
     zl_s, zr_s, low_r, da_s, da_r, db_s, db_r, a_sem, t_sem, o_sem) = rest[bits:]
    r = lax.axis_index("row")
    c = lax.axis_index("col")
    width = bh.shape[2]
    depth = bh.shape[1]
    rows = y.shape[1]
    end = n_cols - 1
    core = lax.rem(r, 2)
    left, right = {"col": c - 1}, {"col": c + 1}
    strip = rows // 4
    kc = abuf.shape[2]
    ch = kc // 4
    n_ch = depth // ch
    piece = strip >> (bits - 1)
    sub = min(piece, 128)
    per = piece // sub
    n_sub = 2 * per

    def bit_of(j):
        if j == 0:
            return 1
        return (1 << j) + core * ((1 << (bits - j)) - (1 << j))

    value = [lax.rem(lax.div(r, bit_of(j)), 2) for j in range(bits)]
    partner = [r + (1 - 2 * value[j]) * bit_of(j) for j in range(bits)]

    def span(start, size):
        return pl.ds(pl.multiple_of(start, 8), size)

    def chunk(k):
        return span(k * ch, ch)

    def remote(src, dst, send, recv, where):
        return pltpu.make_async_remote_copy(
            src_ref=src, dst_ref=dst, send_sem=send, recv_sem=recv,
            device_id=where, device_id_type=MESH,
        )

    def loop(low_, high_, body):
        def step(i, carry):
            body(i)
            return carry
        lax.fori_loop(low_, high_, step, 0)

    def lead_copy(k):
        ref = lead.at[chunk(k), :]
        return remote(ref, ref, lead_s.at[k], lead_r.at[k], left)

    def plus_copy(k):
        ref = plus.at[chunk(k), :]
        return remote(ref, ref, plus_s.at[k], plus_r.at[k], right)

    def minus_copy(k):
        ref = minus.at[chunk(k), :]
        return remote(ref, ref, minus_s.at[k], minus_r.at[k], left)

    lead_at = jnp.where(slot_ref[0] == end, 0, 1)

    def live(s, block):
        at_ = lead_at if s == 0 else 1 - lead_at
        return pattern_ref[at_, block].astype(F32)

    def own(s, k):
        block = lax.div(r * depth + k * ch, width)
        at_ = lead_at if s == 0 else 1 - lead_at
        here = jnp.where(slot_ref[at_] == c, 1.0, 0.0)
        return (live(s, block) * here) * panel[chunk(k), :]

    def keep(s, k, x):
        high, rest_ = halves(x)
        bh[s, chunk(k), :] = high
        bl[s, chunk(k), :] = rest_

    def plus_step(k):
        @pl.when(c > 0)
        def _():
            plus_copy(k).wait_recv()
            plus[chunk(k), :] = plus[chunk(k), :] + own(1, k)

        @pl.when(c == 0)
        def _():
            plus[chunk(k), :] = own(1, k)

        @pl.when(c < end)
        def _():
            plus_copy(k).start()

    def lead_step(k):
        @pl.when(c < end)
        def _():
            lead_copy(k).wait_recv()

        @pl.when(c == end)
        def _():
            lead[chunk(k), :] = own(0, k)

        @pl.when(c > 0)
        def _():
            lead_copy(k).start()
        keep(0, k, lead[chunk(k), :])

    def minus_step(k):
        @pl.when(c < end - 1)
        def _():
            minus_copy(k).wait_recv()
            minus[chunk(k), :] = minus[chunk(k), :] + own(1, k)

        @pl.when(c == end - 1)
        def _():
            minus[chunk(k), :] = own(1, k)

        @pl.when((c > 0) & (c < end))
        def _():
            minus_copy(k).start()

        @pl.when(c < end)
        def _():
            keep(1, k, (plus[chunk(k), :] + minus[chunk(k), :]) - own(1, k))

        @pl.when(c == end)
        def _():
            keep(1, k, plus[chunk(k), :])

    def quarter_start(q):
        half = (1 - value[0]) + lax.rem(q, 2) * (2 * value[0] - 1)
        return half * (rows // 2) + lax.div(q, 2) * strip

    def a_copy(m):
        k = lax.div(lax.rem(m, n_ch), 4)
        slot = lax.rem(m, ABUF)
        return pltpu.make_async_copy(
            a_ref.at[span(quarter_start(lax.rem(m, 4)), strip),
                     pl.ds(pl.multiple_of(k * kc, 128), kc)],
            abuf.at[slot], a_sem.at[slot],
        )

    tall = min(strip, 1024)

    def multiply(m):
        @pl.when(m + ABUF - 1 < 2 * n_ch)
        def _():
            a_copy(m + ABUF - 1).start()

        a_copy(m).wait()
        s = lax.div(m, n_ch)
        k = lax.div(lax.rem(m, n_ch), 4)
        slot = lax.rem(m, ABUF)
        start = quarter_start(lax.rem(m, 4))
        deep = pl.ds(pl.multiple_of(k * kc, 16), kc)

        def body(i):
            a = halves(abuf[slot, span(i * tall, tall), :])
            here = span(start + i * tall, tall)
            part[s, here, :] = part[s, here, :] + dot3(a, (bh[s, deep, :], bl[s, deep, :]))
        loop(0, strip // tall, body)

    def reduce_events(s, h):
        g = 2 * s + h
        src, dst = part.at[s], y.at[s]
        size = [None] + [strip >> j for j in range(bits)]
        start = [None, value[0] * (rows // 2) + h * strip]
        for j in range(1, bits):
            start.append(start[-1] + value[j] * size[j + 1])

        def away(j):
            if j == 0:
                return (1 - value[0]) * (rows // 2) + h * strip
            return start[j] + (1 - value[j]) * size[j + 1]

        def rs(j):
            return remote(src.at[span(away(j), size[j + 1]), :], rs_buf[j].at[g],
                          rs_s.at[g, j], rs_r.at[g, j], {"row": partner[j]})

        def ag(j):
            mine = span(start[1], size[1]) if j == 0 else span(start[j + 1], size[j + 1])
            return remote(dst.at[mine, :], dst.at[mine, :],
                          ag_s.at[g, j], ag_r.at[g, j], {"row": partner[j]})

        def add(j):
            rs(j).wait()
            mine = size[j + 1]
            step = min(mine, 128)

            def body(i):
                here = span(start[j + 1] + i * step, step)
                there = span(i * step, step)
                total = src[here, :] + rs_buf[j][g, there, :]
                if j == bits - 1:
                    block = lax.div(c * rows + start[j + 1] + i * step, width)
                    dst[here, :] = -live(s, block) * total
                else:
                    src[here, :] = total
            loop(0, mine // step, body)

        def cut(copy, i):
            size_ = strip // 8
            here = span(away(0) + i * size_, size_)
            mine = span(start[1] + i * size_, size_)
            if copy is rs:
                remote(src.at[here, :], rs_buf[0].at[g, span(i * size_, size_), :],
                       rs_s.at[g, 0], rs_r.at[g, 0], {"row": partner[0]}).start()
            else:
                remote(dst.at[mine, :], dst.at[mine, :],
                       ag_s.at[g, 0], ag_r.at[g, 0], {"row": partner[0]}).start()

        def event(i):
            if i < bits:
                add(i - 1)
                rs(i).start()
            elif i == bits:
                add(bits - 1)
                ag(bits - 1).start()
            else:
                j = 2 * bits - i
                ag(j).wait()
                if j > 1:
                    ag(j - 1).start()
        return [[functools.partial(cut, f, i) for i in range(8)] for f in (rs, ag)] + [
            functools.partial(event, i) for i in range(1, 2 * bits + 1)]

    def share_start(u):
        start = value[0] * (rows // 2) + (u // per) * strip + (u % per) * sub
        for j in range(1, bits):
            start = start + value[j] * (strip >> j)
        return start

    source = lax.div(r * n_cols, n_rows)
    own_start = r * depth - source * rows

    def target(s, u, plane, to_plane, src, send):
        at = plane * rows + share_start(u)
        to = lax.div(at, depth)
        offset = at - to * depth
        here, recv = low.at[s, span(offset, sub), :], low_r.at[s, lax.div(offset, sub)]
        return to, here, recv, remote(src, here, send, recv, {"row": to, "col": to_plane})

    def share(s, u):
        return y.at[s, span(share_start(u), sub), :]

    def z_copy(s, u, d, way):
        sem = zl_s if way < 0 else zr_s
        return target(s, u, c, c + way * d, share(s, u), sem.at[s, u, d])[3]

    def z_all(s, u, way, act):
        for d in range(end, 0, -1):
            @pl.when((c >= d) if way < 0 else (c + d <= end))
            def _(d=d):
                act(z_copy(s, u, d, way))

    def z_send(s, u, way):
        z_all(s, u, way, lambda copy: copy.start())

    def low_wait(s, i):
        here = low.at[s, span(i * sub, sub), :]
        pltpu.make_async_copy(here, here, low_r.at[s, i]).wait()

    def low_copy(s, i):
        here = span(i * sub, sub)
        return pltpu.make_async_copy(low.at[s, here, :], low_out.at[s, here, :], o_sem.at[s, i])

    def places(u):
        h, k = u // per, u % per
        return [a * (rows // 2) + h * strip + p * piece + k * sub
                for a in range(depth // (rows // 2)) for p in range(strip // piece)]

    def from_y(s, h):
        @pl.when(c == source)
        def _():
            for u in range(h * per, (h + 1) * per):
                for offset in places(u):
                    pltpu.make_async_copy(
                        y.at[s, span(own_start + offset, sub), :],
                        low.at[s, span(offset, sub), :], low_r.at[s, offset // sub],
                    ).start()

    def consume(s, u):
        def one(offset):
            i = lax.div(offset, sub)
            low_wait(s, i)
            here = span(offset, sub)
            low_copy(s, i).start()
            dpart[s] += dot3((bh[s, here, :], bl[s, here, :]), halves(low[s, here, :]),
                             (((0,), (0,)), ((), ())))
        for offset in places(u):
            one(offset)

    ds = width // n_rows

    def other(i):
        return lax.rem(r + i, n_rows)

    def da_copy(s, i, p):
        return remote(dpart.at[s, span(p * ds, ds), :], dbuf.at[s, i],
                      da_s.at[s, p], da_r.at[s, i], {"row": p})

    def db_copy(s, i, p):
        here = dsum.at[s, span(i * ds, ds), :]
        return remote(here, here, db_s.at[s, p], db_r.at[s, i], {"row": p})

    def diag_a(s):
        loop(1, n_rows, lambda i: da_copy(s, r, other(i)).start())

    def diag_b(s):
        mine = span(r * ds, ds)
        dsum[s, mine, :] = dpart[s, mine, :]

        def body(i):
            da_copy(s, other(i), other(i)).wait_recv()
            dsum[s, mine, :] += dbuf[s, other(i)]
        loop(1, n_rows, body)
        loop(1, n_rows, lambda i: db_copy(s, r, other(i)).start())

    def diag_c(s):
        loop(1, n_rows, lambda i: db_copy(s, other(i), other(i)).wait_recv())
        diag_out[s] = dsum[s]

    tb = rows // 8

    def turn_copy(i):
        s, b = i // 8, i % 8
        return pltpu.make_async_copy(
            turned.at[b], y_out.at[s, :, pl.ds(b * tb, tb)], t_sem.at[b]
        )

    def turn(i):
        s, b = i // 8, i % 8
        if s > 0:
            turn_copy(i - 8).wait()
        turned[b] = y[s, pl.ds(b * tb, tb), :].T
        turn_copy(i).start()

    events = []

    def at(time, f, *args):
        events.append((time, len(events), functools.partial(f, *args)))

    full = 2 * n_ch
    for s in range(2):
        b = n_ch * (s + 1)
        for h in range(2):
            out, back, *steps = reduce_events(s, h)
            when = [b + 5 + 4 * h] if s == 0 else [b + 4 + 2 * h]
            when += [b + 11 + 5 * (j - 2) + 4 * h for j in range(2, bits + 1)]
            last = when[-1]
            when += [last + 5 + 6 * j for j in range(bits)]
            for n, f in enumerate(out):
                at(b - 1 + 4 * h + n // 2 if s == 0 else b - 1 + 2 * h, f)
            for n, f in enumerate(back):
                at(when[-2] + (n // 2 if s == 0 else 0) + 0.25, f)
            for time, f in zip(when, steps):
                at(time, f)
            for u in range(h * per, (h + 1) * per):
                at(last + (4 if s == 0 else 0), z_send, s, u, 1)
                at(max(full - 1, last), z_send, s, u, -1)
            at(when[-1], from_y, s, h)
        done = when[-1]
        for i in range(8):
            at(max(full + (25.5 if s == 0 else 0), done + 0.5) + i / 8, turn, 8 * s + i)
        final = max(full + 28, done) if s == 0 else full + 50
        for u in range(n_sub):
            at(final + u / n_sub, consume, s, u)
        at(final + 1, diag_a, s)
        at(full + (49 if s == 0 else 52), diag_b, s)
        at(full + 53, diag_c, s)
    events.sort(key=lambda e: e[:2])

    barrier = pltpu.get_barrier_semaphore()
    loop(1, n_rows, lambda i: pl.semaphore_signal(
        barrier, inc=1, device_id={"row": other(i)}, device_id_type=MESH))

    @pl.when(c > 0)
    def _():
        pl.semaphore_signal(barrier, inc=1, device_id=left, device_id_type=MESH)

    @pl.when(c < end)
    def _():
        pl.semaphore_signal(barrier, inc=1, device_id=right, device_id_type=MESH)

    for m in range(ABUF - 1):
        a_copy(m).start()
    dpart[...] = jnp.zeros_like(dpart)

    def clear(i):
        for s in range(2):
            part[s, span(i * strip // 4, strip // 4), :] = jnp.zeros((strip // 4, width), F32)
    loop(0, 16, clear)

    beside = lax.div(c + end - 1, end) + lax.div(2 * end - 1 - c, end)
    pl.semaphore_wait(barrier, n_rows - 1 + beside)

    stop = 2 * n_ch + LAG
    inside = [e for e in events if e[0] < stop]
    outside = [e for e in events if e[0] >= stop]
    times = sorted({e[0] for e in inside})

    def body(u):
        up = u + AHEAD * (end - 2 * c)

        @pl.when((up >= 0) & (up < n_ch))
        def _():
            plus_step(up)

        @pl.when((u >= 0) & (u < n_ch))
        def _():
            lead_step(u)

        @pl.when((u >= n_ch) & (u < 2 * n_ch))
        def _():
            minus_step(u - n_ch)

        @pl.when((u >= LAG) & (u < 2 * n_ch + LAG))
        def _():
            multiply(u - LAG)

        for time in times:
            @pl.when(u == int(time))
            def _(time=time):
                for e in inside:
                    if e[0] == time:
                        e[2]()
    loop(-AHEAD * (end - c), stop, body)
    for e in outside:
        e[2]()

    def drain_panel(k):
        @pl.when(c > 0)
        def _():
            lead_copy(k).wait_send()

        @pl.when((c > 0) & (c < end))
        def _():
            minus_copy(k).wait_send()

        @pl.when(c < end)
        def _():
            plus_copy(k).wait_send()
    loop(0, n_ch, drain_panel)

    for s in range(2):
        for u in range(n_sub):
            for way in (-1, 1):
                z_all(s, u, way, lambda copy: copy.wait_send())
        loop(1, n_rows, lambda i: da_copy(s, r, other(i)).wait_send())
        loop(1, n_rows, lambda i: db_copy(s, r, other(i)).wait_send())
        loop(0, depth // sub, lambda i: low_copy(s, i).wait())
    for i in range(8, 16):
        turn_copy(i).wait()


def exchange(n_rows, n_cols, a, panel, pattern, slots):
    rows, depth = a.shape
    width = panel.shape[1]
    bits = n_rows.bit_length() - 1
    vmem = pl.BlockSpec(memory_space=pltpu.VMEM)
    smem = pl.BlockSpec(memory_space=pltpu.SMEM)
    anywhere = pl.BlockSpec(memory_space=pl.ANY)
    dma = pltpu.SemaphoreType.DMA
    kc = min(256, depth)
    n = depth // (kc // 4)
    strip = rows // 4
    piece = strip >> (bits - 1)
    sub = min(piece, 128)
    n_sub = 2 * piece // sub
    return pl.pallas_call(
        functools.partial(kernel, n_rows, n_cols),
        out_shape=(
            jax.ShapeDtypeStruct((2, width, rows), F32),
            jax.ShapeDtypeStruct((2, depth, width), F32),
            jax.ShapeDtypeStruct((2, width, width), F32),
        ),
        in_specs=[anywhere, vmem, smem, smem],
        out_specs=(anywhere, anywhere, vmem),
        scratch_shapes=[
            pltpu.VMEM((2, depth, width), BF16),
            pltpu.VMEM((2, depth, width), BF16),
            pltpu.VMEM((depth, width), F32),
            pltpu.VMEM((depth, width), F32),
            pltpu.VMEM((depth, width), F32),
            pltpu.VMEM((2, rows, width), F32),
            pltpu.VMEM((2, rows, width), F32),
            pltpu.VMEM((2, depth, width), F32),
            pltpu.VMEM((ABUF, strip, kc), F32),
            pltpu.VMEM((8, width, rows // 8), F32),
            pltpu.VMEM((2, width, width), F32),
            pltpu.VMEM((2, n_rows, width // n_rows, width), F32),
            pltpu.VMEM((2, width, width), F32),
            *[pltpu.VMEM((4, strip >> j, width), F32) for j in range(bits)],
            dma((n,)), dma((n,)), dma((n,)), dma((n,)), dma((n,)), dma((n,)),
            dma((4, bits)), dma((4, bits)), dma((4, bits)), dma((4, bits)),
            dma((2, n_sub, n_cols)), dma((2, n_sub, n_cols)),
            dma((2, depth // sub)),
            dma((2, n_rows)), dma((2, n_rows)), dma((2, n_rows)), dma((2, n_rows)),
            dma((ABUF,)), dma((8,)), dma((2, depth // sub)),
        ],
        compiler_params=pltpu.CompilerParams(
            collective_id=0, has_side_effects=True, vmem_limit_bytes=66_000_000
        ),
    )(a, panel, pattern, slots)


def settle_kernel(slots, y_in, low_in, dsum, dinv, y_out, low_out, diag_out):
    y_out[...] = y_in[...]
    low_out[...] = low_in[...]
    diag_out[...] = dinv[...] - dsum[...]


def settle(n_cols, slots, y, low, dsum, dinv):
    parts = 4

    def spec(x, moved):
        block = (1, x.shape[1] // parts, x.shape[2])
        if moved:
            return pl.BlockSpec(block, lambda s, p, slots: (
                jnp.where(slots[0] == n_cols - 1, s, 1 - s), p, 0))
        return pl.BlockSpec(block, lambda s, p, slots: (s, p, 0))
    outs = (y, low, dinv)
    return pl.pallas_call(
        settle_kernel,
        out_shape=tuple(jax.ShapeDtypeStruct(x.shape, F32) for x in outs),
        grid_spec=pltpu.PrefetchScalarGridSpec(
            num_scalar_prefetch=1, grid=(2, parts),
            in_specs=[spec(y, True), spec(low, True), spec(dsum, True), spec(dinv, False)],
            out_specs=tuple(spec(x, False) for x in outs),
        ),
    )(slots, y, low, dsum, dinv)


def shards(inverse_rows, panels, diag_inverse, pattern, owner_slot):
    n_rows, n_cols = lax.axis_size("row"), lax.axis_size("col")
    y, low, dsum = exchange(n_rows, n_cols, inverse_rows, panels[0], pattern, owner_slot)
    y, low, diag = settle(n_cols, owner_slot, y, low, dsum, diag_inverse)
    return low, y, diag


def solution(mesh):
    in_specs = (P("col", "row"), P("col", "row", None), P(), P(), P())
    out_specs = (P(None, "row", None), P(None, None, "col"), P())
    return jax.shard_map(shards, mesh=mesh, in_specs=in_specs, out_specs=out_specs, check_vma=False)
```

```python
import functools

import jax
import jax.numpy as jnp
from jax import lax
from jax.experimental import pallas as pl
from jax.experimental.pallas import tpu as pltpu
from jax.sharding import PartitionSpec as P

MESH = pl.DeviceIdType.MESH
F32 = jnp.float32
BF16 = jnp.bfloat16
AHEAD = 3
LAG = 3
ABUF = 4


def halves(x):
    high = x.astype(BF16)
    return high, (x - high.astype(F32)).astype(BF16)


def dot3(a, b, dims=(((1,), (0,)), ((), ()))):
    (ah, al), (bh, bl) = a, b
    dot = functools.partial(lax.dot_general, dimension_numbers=dims, preferred_element_type=F32)
    return dot(ah, bh) + dot(ah, bl) + dot(al, bh)


def kernel(
    n_rows, n_cols,
    a_ref, panel, pattern_ref, slot_ref,
    y_out, low_out, diag_out,
    bh, bl, lead, plus, minus, part, y, low, abuf, turned, dpart, dbuf, dsum, *rest,
):
    bits = n_rows.bit_length() - 1
    rs_buf = rest[:bits]
    (lead_s, lead_r, plus_s, plus_r, minus_s, minus_r, rs_s, rs_r, ag_s, ag_r,
     zl_s, zr_s, low_r, da_s, da_r, db_s, db_r, a_sem, t_sem, o_sem) = rest[bits:]
    r = lax.axis_index("row")
    c = lax.axis_index("col")
    width = bh.shape[2]
    depth = bh.shape[1]
    rows = y.shape[1]
    end = n_cols - 1
    core = lax.rem(r, 2)
    left, right = {"col": c - 1}, {"col": c + 1}
    strip = rows // 4
    kc = abuf.shape[2]
    ch = kc // 4
    n_ch = depth // ch
    piece = strip >> (bits - 1)
    sub = min(piece, 128)
    per = piece // sub
    n_sub = 2 * per

    def bit_of(j):
        if j == 0:
            return 1
        return (1 << j) + core * ((1 << (bits - j)) - (1 << j))

    value = [lax.rem(lax.div(r, bit_of(j)), 2) for j in range(bits)]
    partner = [r + (1 - 2 * value[j]) * bit_of(j) for j in range(bits)]

    def span(start, size):
        return pl.ds(pl.multiple_of(start, 8), size)

    def chunk(k):
        return span(k * ch, ch)

    def remote(src, dst, send, recv, where):
        return pltpu.make_async_remote_copy(
            src_ref=src, dst_ref=dst, send_sem=send, recv_sem=recv,
            device_id=where, device_id_type=MESH,
        )

    def loop(low_, high_, body):
        def step(i, carry):
            body(i)
            return carry
        lax.fori_loop(low_, high_, step, 0)

    def lead_copy(k):
        ref = lead.at[chunk(k), :]
        return remote(ref, ref, lead_s.at[k], lead_r.at[k], left)

    def plus_copy(k):
        ref = plus.at[chunk(k), :]
        return remote(ref, ref, plus_s.at[k], plus_r.at[k], right)

    def minus_copy(k):
        ref = minus.at[chunk(k), :]
        return remote(ref, ref, minus_s.at[k], minus_r.at[k], left)

    lead_at = jnp.where(slot_ref[0] == end, 0, 1)

    def live(s, block):
        at_ = lead_at if s == 0 else 1 - lead_at
        return pattern_ref[at_, block].astype(F32)

    def own(s, k):
        block = lax.div(r * depth + k * ch, width)
        at_ = lead_at if s == 0 else 1 - lead_at
        here = jnp.where(slot_ref[at_] == c, 1.0, 0.0)
        return (live(s, block) * here) * panel[chunk(k), :]

    def keep(s, k, x):
        high, rest_ = halves(x)
        bh[s, chunk(k), :] = high
        bl[s, chunk(k), :] = rest_

    def plus_step(k):
        @pl.when(c > 0)
        def _():
            plus_copy(k).wait_recv()
            plus[chunk(k), :] = plus[chunk(k), :] + own(1, k)

        @pl.when(c == 0)
        def _():
            plus[chunk(k), :] = own(1, k)

        @pl.when(c < end)
        def _():
            plus_copy(k).start()

    def lead_step(k):
        @pl.when(c < end)
        def _():
            lead_copy(k).wait_recv()

        @pl.when(c == end)
        def _():
            lead[chunk(k), :] = own(0, k)

        @pl.when(c > 0)
        def _():
            lead_copy(k).start()
        keep(0, k, lead[chunk(k), :])

    def minus_step(k):
        @pl.when(c < end - 1)
        def _():
            minus_copy(k).wait_recv()
            minus[chunk(k), :] = minus[chunk(k), :] + own(1, k)

        @pl.when(c == end - 1)
        def _():
            minus[chunk(k), :] = own(1, k)

        @pl.when((c > 0) & (c < end))
        def _():
            minus_copy(k).start()

        @pl.when(c < end)
        def _():
            keep(1, k, (plus[chunk(k), :] + minus[chunk(k), :]) - own(1, k))

        @pl.when(c == end)
        def _():
            keep(1, k, plus[chunk(k), :])

    def quarter_start(q):
        half = (1 - value[0]) + lax.rem(q, 2) * (2 * value[0] - 1)
        return half * (rows // 2) + lax.div(q, 2) * strip

    def a_copy(m):
        k = lax.div(lax.rem(m, n_ch), 4)
        slot = lax.rem(m, ABUF)
        return pltpu.make_async_copy(
            a_ref.at[span(quarter_start(lax.rem(m, 4)), strip),
                     pl.ds(pl.multiple_of(k * kc, 128), kc)],
            abuf.at[slot], a_sem.at[slot],
        )

    tall = min(strip, 1024)

    def multiply(m):
        @pl.when(m + ABUF - 1 < 2 * n_ch)
        def _():
            a_copy(m + ABUF - 1).start()

        a_copy(m).wait()
        s = lax.div(m, n_ch)
        k = lax.div(lax.rem(m, n_ch), 4)
        slot = lax.rem(m, ABUF)
        start = quarter_start(lax.rem(m, 4))
        deep = pl.ds(pl.multiple_of(k * kc, 16), kc)

        def body(i):
            a = halves(abuf[slot, span(i * tall, tall), :])
            here = span(start + i * tall, tall)
            part[s, here, :] = part[s, here, :] + dot3(a, (bh[s, deep, :], bl[s, deep, :]))
        loop(0, strip // tall, body)

    def reduce_events(s, h):
        g = 2 * s + h
        src, dst = part.at[s], y.at[s]
        size = [None] + [strip >> j for j in range(bits)]
        start = [None, value[0] * (rows // 2) + h * strip]
        for j in range(1, bits):
            start.append(start[-1] + value[j] * size[j + 1])

        def away(j):
            if j == 0:
                return (1 - value[0]) * (rows // 2) + h * strip
            return start[j] + (1 - value[j]) * size[j + 1]

        def rs(j):
            return remote(src.at[span(away(j), size[j + 1]), :], rs_buf[j].at[g],
                          rs_s.at[g, j], rs_r.at[g, j], {"row": partner[j]})

        def ag(j):
            mine = span(start[1], size[1]) if j == 0 else span(start[j + 1], size[j + 1])
            return remote(dst.at[mine, :], dst.at[mine, :],
                          ag_s.at[g, j], ag_r.at[g, j], {"row": partner[j]})

        def add(j):
            rs(j).wait()
            mine = size[j + 1]
            step = min(mine, 128)

            def body(i):
                here = span(start[j + 1] + i * step, step)
                there = span(i * step, step)
                total = src[here, :] + rs_buf[j][g, there, :]
                if j == bits - 1:
                    block = lax.div(c * rows + start[j + 1] + i * step, width)
                    dst[here, :] = -live(s, block) * total
                else:
                    src[here, :] = total
            loop(0, mine // step, body)

        def cut(copy, i):
            size_ = strip // 8
            here = span(away(0) + i * size_, size_)
            mine = span(start[1] + i * size_, size_)
            if copy is rs:
                remote(src.at[here, :], rs_buf[0].at[g, span(i * size_, size_), :],
                       rs_s.at[g, 0], rs_r.at[g, 0], {"row": partner[0]}).start()
            else:
                remote(dst.at[mine, :], dst.at[mine, :],
                       ag_s.at[g, 0], ag_r.at[g, 0], {"row": partner[0]}).start()

        def event(i):
            if i < bits:
                add(i - 1)
                rs(i).start()
            elif i == bits:
                add(bits - 1)
                ag(bits - 1).start()
            else:
                j = 2 * bits - i
                ag(j).wait()
                if j > 1:
                    ag(j - 1).start()
        return [[functools.partial(cut, f, i) for i in range(8)] for f in (rs, ag)] + [
            functools.partial(event, i) for i in range(1, 2 * bits + 1)]

    def share_start(u):
        start = value[0] * (rows // 2) + (u // per) * strip + (u % per) * sub
        for j in range(1, bits):
            start = start + value[j] * (strip >> j)
        return start

    source = lax.div(r * n_cols, n_rows)
    own_start = r * depth - source * rows

    def target(s, u, plane, to_plane, src, send):
        at = plane * rows + share_start(u)
        to = lax.div(at, depth)
        offset = at - to * depth
        here, recv = low.at[s, span(offset, sub), :], low_r.at[s, lax.div(offset, sub)]
        return to, here, recv, remote(src, here, send, recv, {"row": to, "col": to_plane})

    def share(s, u):
        return y.at[s, span(share_start(u), sub), :]

    def z_copy(s, u, d, way):
        sem = zl_s if way < 0 else zr_s
        return target(s, u, c, c + way * d, share(s, u), sem.at[s, u, d])[3]

    def z_all(s, u, way, act):
        for d in range(end, 0, -1):
            @pl.when((c >= d) if way < 0 else (c + d <= end))
            def _(d=d):
                act(z_copy(s, u, d, way))

    def z_send(s, u, way):
        z_all(s, u, way, lambda copy: copy.start())

    def low_wait(s, i):
        here = low.at[s, span(i * sub, sub), :]
        pltpu.make_async_copy(here, here, low_r.at[s, i]).wait()

    def low_copy(s, i):
        here = span(i * sub, sub)
        return pltpu.make_async_copy(low.at[s, here, :], low_out.at[s, here, :], o_sem.at[s, i])

    def places(u):
        h, k = u // per, u % per
        return [a * (rows // 2) + h * strip + p * piece + k * sub
                for a in range(depth // (rows // 2)) for p in range(strip // piece)]

    def from_y(s, h):
        @pl.when(c == source)
        def _():
            for u in range(h * per, (h + 1) * per):
                for offset in places(u):
                    pltpu.make_async_copy(
                        y.at[s, span(own_start + offset, sub), :],
                        low.at[s, span(offset, sub), :], low_r.at[s, offset // sub],
                    ).start()

    def consume(s, u):
        def one(offset):
            i = lax.div(offset, sub)
            low_wait(s, i)
            here = span(offset, sub)
            low_copy(s, i).start()
            dpart[s] += dot3((bh[s, here, :], bl[s, here, :]), halves(low[s, here, :]),
                             (((0,), (0,)), ((), ())))
        for offset in places(u):
            one(offset)

    ds = width // n_rows

    def other(i):
        return lax.rem(r + i, n_rows)

    def da_copy(s, i, p):
        return remote(dpart.at[s, span(p * ds, ds), :], dbuf.at[s, i],
                      da_s.at[s, p], da_r.at[s, i], {"row": p})

    def db_copy(s, i, p):
        here = dsum.at[s, span(i * ds, ds), :]
        return remote(here, here, db_s.at[s, p], db_r.at[s, i], {"row": p})

    def diag_a(s):
        loop(1, n_rows, lambda i: da_copy(s, r, other(i)).start())

    def diag_b(s):
        mine = span(r * ds, ds)
        dsum[s, mine, :] = dpart[s, mine, :]

        def body(i):
            da_copy(s, other(i), other(i)).wait_recv()
            dsum[s, mine, :] += dbuf[s, other(i)]
        loop(1, n_rows, body)
        loop(1, n_rows, lambda i: db_copy(s, r, other(i)).start())

    def diag_c(s):
        loop(1, n_rows, lambda i: db_copy(s, other(i), other(i)).wait_recv())
        diag_out[s] = dsum[s]

    tb = rows // 8

    def turn_copy(i):
        s, b = i // 8, i % 8
        return pltpu.make_async_copy(
            turned.at[b], y_out.at[s, :, pl.ds(b * tb, tb)], t_sem.at[b]
        )

    def turn(i):
        s, b = i // 8, i % 8
        if s > 0:
            turn_copy(i - 8).wait()
        turned[b] = y[s, pl.ds(b * tb, tb), :].T
        turn_copy(i).start()

    events = []

    def at(time, f, *args):
        events.append((time, len(events), functools.partial(f, *args)))

    full = 2 * n_ch
    for s in range(2):
        b = n_ch * (s + 1)
        for h in range(2):
            out, back, *steps = reduce_events(s, h)
            when = [b + 5 + 4 * h] if s == 0 else [b + 4 + 2 * h]
            when += [b + 11 + 5 * (j - 2) + 4 * h for j in range(2, bits + 1)]
            last = when[-1]
            when += [last + 5 + 6 * j for j in range(bits)]
            for n, f in enumerate(out):
                at(b - 1 + 4 * h + n // 2 if s == 0 else b - 1 + 2 * h, f)
            for n, f in enumerate(back):
                at(when[-2] + (n // 2 if s == 0 else 0) + 0.25, f)
            for time, f in zip(when, steps):
                at(time, f)
            for u in range(h * per, (h + 1) * per):
                at(last + (4 if s == 0 else 0), z_send, s, u, 1)
                at(max(full - 1, last), z_send, s, u, -1)
            at(when[-1], from_y, s, h)
        done = when[-1]
        for i in range(8):
            at(max(full + (25.5 if s == 0 else 0), done + 0.5) + i / 8, turn, 8 * s + i)
        final = max(full + 28, done) if s == 0 else full + 50
        for u in range(n_sub):
            at(final + u / n_sub, consume, s, u)
        at(final + 1, diag_a, s)
        at(full + (49 if s == 0 else 52), diag_b, s)
        at(full + 53, diag_c, s)
    events.sort(key=lambda e: e[:2])

    barrier = pltpu.get_barrier_semaphore()
    loop(1, n_rows, lambda i: pl.semaphore_signal(
        barrier, inc=1, device_id={"row": other(i)}, device_id_type=MESH))

    @pl.when(c > 0)
    def _():
        pl.semaphore_signal(barrier, inc=1, device_id=left, device_id_type=MESH)

    @pl.when(c < end)
    def _():
        pl.semaphore_signal(barrier, inc=1, device_id=right, device_id_type=MESH)

    for m in range(ABUF - 1):
        a_copy(m).start()
    dpart[...] = jnp.zeros_like(dpart)

    def clear(i):
        for s in range(2):
            part[s, span(i * strip // 4, strip // 4), :] = jnp.zeros((strip // 4, width), F32)
    loop(0, 16, clear)

    beside = lax.div(c + end - 1, end) + lax.div(2 * end - 1 - c, end)
    pl.semaphore_wait(barrier, n_rows - 1 + beside)

    stop = 2 * n_ch + LAG
    inside = [e for e in events if e[0] < stop]
    outside = [e for e in events if e[0] >= stop]
    times = sorted({e[0] for e in inside})

    def body(u):
        up = u + AHEAD * (end - 2 * c)

        @pl.when((up >= 0) & (up < n_ch))
        def _():
            plus_step(up)

        @pl.when((u >= 0) & (u < n_ch))
        def _():
            lead_step(u)

        @pl.when((u >= n_ch) & (u < 2 * n_ch))
        def _():
            minus_step(u - n_ch)

        @pl.when((u >= LAG) & (u < 2 * n_ch + LAG))
        def _():
            multiply(u - LAG)

        for time in times:
            @pl.when(u == int(time))
            def _(time=time):
                for e in inside:
                    if e[0] == time:
                        e[2]()
    loop(-AHEAD * (end - c), stop, body)
    for e in outside:
        e[2]()

    def drain_panel(k):
        @pl.when(c > 0)
        def _():
            lead_copy(k).wait_send()

        @pl.when((c > 0) & (c < end))
        def _():
            minus_copy(k).wait_send()

        @pl.when(c < end)
        def _():
            plus_copy(k).wait_send()
    loop(0, n_ch, drain_panel)

    for s in range(2):
        for u in range(n_sub):
            for way in (-1, 1):
                z_all(s, u, way, lambda copy: copy.wait_send())
        loop(1, n_rows, lambda i: da_copy(s, r, other(i)).wait_send())
        loop(1, n_rows, lambda i: db_copy(s, r, other(i)).wait_send())
        loop(0, depth // sub, lambda i: low_copy(s, i).wait())
    for i in range(8, 16):
        turn_copy(i).wait()


def exchange(n_rows, n_cols, a, panel, pattern, slots):
    rows, depth = a.shape
    width = panel.shape[1]
    bits = n_rows.bit_length() - 1
    vmem = pl.BlockSpec(memory_space=pltpu.VMEM)
    smem = pl.BlockSpec(memory_space=pltpu.SMEM)
    anywhere = pl.BlockSpec(memory_space=pl.ANY)
    dma = pltpu.SemaphoreType.DMA
    kc = min(256, depth)
    n = depth // (kc // 4)
    strip = rows // 4
    piece = strip >> (bits - 1)
    sub = min(piece, 128)
    n_sub = 2 * piece // sub
    return pl.pallas_call(
        functools.partial(kernel, n_rows, n_cols),
        out_shape=(
            jax.ShapeDtypeStruct((2, width, rows), F32),
            jax.ShapeDtypeStruct((2, depth, width), F32),
            jax.ShapeDtypeStruct((2, width, width), F32),
        ),
        in_specs=[anywhere, vmem, smem, smem],
        out_specs=(anywhere, anywhere, vmem),
        scratch_shapes=[
            pltpu.VMEM((2, depth, width), BF16),
            pltpu.VMEM((2, depth, width), BF16),
            pltpu.VMEM((depth, width), F32),
            pltpu.VMEM((depth, width), F32),
            pltpu.VMEM((depth, width), F32),
            pltpu.VMEM((2, rows, width), F32),
            pltpu.VMEM((2, rows, width), F32),
            pltpu.VMEM((2, depth, width), F32),
            pltpu.VMEM((ABUF, strip, kc), F32),
            pltpu.VMEM((8, width, rows // 8), F32),
            pltpu.VMEM((2, width, width), F32),
            pltpu.VMEM((2, n_rows, width // n_rows, width), F32),
            pltpu.VMEM((2, width, width), F32),
            *[pltpu.VMEM((4, strip >> j, width), F32) for j in range(bits)],
            dma((n,)), dma((n,)), dma((n,)), dma((n,)), dma((n,)), dma((n,)),
            dma((4, bits)), dma((4, bits)), dma((4, bits)), dma((4, bits)),
            dma((2, n_sub, n_cols)), dma((2, n_sub, n_cols)),
            dma((2, depth // sub)),
            dma((2, n_rows)), dma((2, n_rows)), dma((2, n_rows)), dma((2, n_rows)),
            dma((ABUF,)), dma((8,)), dma((2, depth // sub)),
        ],
        compiler_params=pltpu.CompilerParams(
            collective_id=0, has_side_effects=True, vmem_limit_bytes=66_000_000
        ),
    )(a, panel, pattern, slots)


def settle_kernel(
    end, slots, y_in, low_in, dsum, dinv, y_out, low_out, diag_out, y_buf, low_buf, in_sem, out_sem
):
    lead_at = jnp.where(slots[0] == end, 0, 1)
    moves = []
    for s, at in ((0, lead_at), (1, 1 - lead_at)):
        for src, buf, dst, parts in ((y_in, y_buf, y_out, 4), (low_in, low_buf, low_out, 2)):
            size = buf.shape[1] // parts
            for p in range(parts):
                here, n = pl.ds(p * size, size), len(moves)
                moves.append((
                    pltpu.make_async_copy(src.at[at, here, :], buf.at[s, here, :], in_sem.at[n]),
                    pltpu.make_async_copy(buf.at[s, here, :], dst.at[s, here, :], out_sem.at[n]),
                ))
    for load, _ in moves:
        load.start()
    diag_out[0] = dinv[0] - dsum[lead_at]
    diag_out[1] = dinv[1] - dsum[1 - lead_at]
    for load, store in moves:
        load.wait()
        store.start()
    for _, store in moves:
        store.wait()


def settle(n_cols, slots, y, low, dsum, dinv):
    vmem = pl.BlockSpec(memory_space=pltpu.VMEM)
    smem = pl.BlockSpec(memory_space=pltpu.SMEM)
    anywhere = pl.BlockSpec(memory_space=pl.ANY)
    return pl.pallas_call(
        functools.partial(settle_kernel, n_cols - 1),
        out_shape=tuple(jax.ShapeDtypeStruct(x.shape, F32) for x in (y, low, dinv)),
        in_specs=[smem, anywhere, anywhere, vmem, vmem],
        out_specs=(anywhere, anywhere, vmem),
        scratch_shapes=[
            pltpu.VMEM(y.shape, F32), pltpu.VMEM(low.shape, F32),
            pltpu.SemaphoreType.DMA((12,)), pltpu.SemaphoreType.DMA((12,)),
        ],
        compiler_params=pltpu.CompilerParams(vmem_limit_bytes=40_000_000),
    )(slots, y, low, dsum, dinv)


def shards(inverse_rows, panels, diag_inverse, pattern, owner_slot):
    n_rows, n_cols = lax.axis_size("row"), lax.axis_size("col")
    y, low, dsum = exchange(n_rows, n_cols, inverse_rows, panels[0], pattern, owner_slot)
    y, low, diag = settle(n_cols, owner_slot, y, low, dsum, diag_inverse)
    return low, y, diag


def solution(mesh):
    in_specs = (P("col", "row"), P("col", "row", None), P(), P(), P())
    out_specs = (P(None, "row", None), P(None, None, "col"), P())
    return jax.shard_map(shards, mesh=mesh, in_specs=in_specs, out_specs=out_specs, check_vma=False)
```

```python
import functools

import jax
import jax.numpy as jnp
from jax import lax
from jax.experimental import pallas as pl
from jax.experimental.pallas import tpu as pltpu
from jax.sharding import PartitionSpec as P

MESH = pl.DeviceIdType.MESH
F32 = jnp.float32
BF16 = jnp.bfloat16
AHEAD = 3
LAG = 3
ABUF = 4


def halves(x):
    high = x.astype(BF16)
    return high, (x - high.astype(F32)).astype(BF16)


def dot3(a, b, dims=(((1,), (0,)), ((), ()))):
    (ah, al), (bh, bl) = a, b
    dot = functools.partial(lax.dot_general, dimension_numbers=dims, preferred_element_type=F32)
    return dot(ah, bh) + dot(ah, bl) + dot(al, bh)


def kernel(
    n_rows, n_cols,
    a_ref, panel, pattern_ref, slot_ref,
    y_out, low_out, diag_out,
    bh, bl, lead, plus, minus, part, y, low, abuf, turned, dpart, dbuf, dsum, *rest,
):
    bits = n_rows.bit_length() - 1
    rs_buf = rest[:bits]
    (lead_s, lead_r, plus_s, plus_r, minus_s, minus_r, rs_s, rs_r, ag_s, ag_r,
     zl_s, zr_s, low_r, da_s, da_r, db_s, db_r, a_sem, t_sem, o_sem) = rest[bits:]
    r = lax.axis_index("row")
    c = lax.axis_index("col")
    width = bh.shape[2]
    depth = bh.shape[1]
    rows = y.shape[1]
    end = n_cols - 1
    core = lax.rem(r, 2)
    left, right = {"col": c - 1}, {"col": c + 1}
    strip = rows // 4
    kc = abuf.shape[2]
    ch = kc // 4
    n_ch = depth // ch
    piece = strip >> (bits - 1)
    sub = min(piece, 128)
    per = piece // sub
    n_sub = 2 * per

    def bit_of(j):
        if j == 0:
            return 1
        return (1 << j) + core * ((1 << (bits - j)) - (1 << j))

    value = [lax.rem(lax.div(r, bit_of(j)), 2) for j in range(bits)]
    partner = [r + (1 - 2 * value[j]) * bit_of(j) for j in range(bits)]

    def span(start, size):
        return pl.ds(pl.multiple_of(start, 8), size)

    def chunk(k):
        return span(k * ch, ch)

    def remote(src, dst, send, recv, where):
        return pltpu.make_async_remote_copy(
            src_ref=src, dst_ref=dst, send_sem=send, recv_sem=recv,
            device_id=where, device_id_type=MESH,
        )

    def loop(low_, high_, body):
        def step(i, carry):
            body(i)
            return carry
        lax.fori_loop(low_, high_, step, 0)

    def lead_copy(k):
        ref = lead.at[chunk(k), :]
        return remote(ref, ref, lead_s.at[k], lead_r.at[k], left)

    def plus_copy(k):
        ref = plus.at[chunk(k), :]
        return remote(ref, ref, plus_s.at[k], plus_r.at[k], right)

    def minus_copy(k):
        ref = minus.at[chunk(k), :]
        return remote(ref, ref, minus_s.at[k], minus_r.at[k], left)

    lead_at = jnp.where(slot_ref[0] == end, 0, 1)

    def live(s, block):
        at_ = lead_at if s == 0 else 1 - lead_at
        return pattern_ref[at_, block].astype(F32)

    def own(s, k):
        block = lax.div(r * depth + k * ch, width)
        at_ = lead_at if s == 0 else 1 - lead_at
        here = jnp.where(slot_ref[at_] == c, 1.0, 0.0)
        return (live(s, block) * here) * panel[chunk(k), :]

    def keep(s, k, x):
        high, rest_ = halves(x)
        bh[s, chunk(k), :] = high
        bl[s, chunk(k), :] = rest_

    def plus_step(k):
        @pl.when(c > 0)
        def _():
            plus_copy(k).wait_recv()
            plus[chunk(k), :] = plus[chunk(k), :] + own(1, k)

        @pl.when(c == 0)
        def _():
            plus[chunk(k), :] = own(1, k)

        @pl.when(c < end)
        def _():
            plus_copy(k).start()

    def lead_step(k):
        @pl.when(c < end)
        def _():
            lead_copy(k).wait_recv()

        @pl.when(c == end)
        def _():
            lead[chunk(k), :] = own(0, k)

        @pl.when(c > 0)
        def _():
            lead_copy(k).start()
        keep(0, k, lead[chunk(k), :])

    def minus_step(k):
        @pl.when(c < end - 1)
        def _():
            minus_copy(k).wait_recv()
            minus[chunk(k), :] = minus[chunk(k), :] + own(1, k)

        @pl.when(c == end - 1)
        def _():
            minus[chunk(k), :] = own(1, k)

        @pl.when((c > 0) & (c < end))
        def _():
            minus_copy(k).start()

        @pl.when(c < end)
        def _():
            keep(1, k, (plus[chunk(k), :] + minus[chunk(k), :]) - own(1, k))

        @pl.when(c == end)
        def _():
            keep(1, k, plus[chunk(k), :])

    def quarter_start(q):
        half = (1 - value[0]) + lax.rem(q, 2) * (2 * value[0] - 1)
        return half * (rows // 2) + lax.div(q, 2) * strip

    def a_copy(m):
        k = lax.div(lax.rem(m, n_ch), 4)
        slot = lax.rem(m, ABUF)
        return pltpu.make_async_copy(
            a_ref.at[span(quarter_start(lax.rem(m, 4)), strip),
                     pl.ds(pl.multiple_of(k * kc, 128), kc)],
            abuf.at[slot], a_sem.at[slot],
        )

    tall = min(strip, 1024)

    def multiply(m):
        @pl.when(m + ABUF - 1 < 2 * n_ch)
        def _():
            a_copy(m + ABUF - 1).start()

        a_copy(m).wait()
        s = lax.div(m, n_ch)
        k = lax.div(lax.rem(m, n_ch), 4)
        slot = lax.rem(m, ABUF)
        start = quarter_start(lax.rem(m, 4))
        deep = pl.ds(pl.multiple_of(k * kc, 16), kc)

        def body(i):
            a = halves(abuf[slot, span(i * tall, tall), :])
            here = span(start + i * tall, tall)
            part[s, here, :] = part[s, here, :] + dot3(a, (bh[s, deep, :], bl[s, deep, :]))
        loop(0, strip // tall, body)

    def reduce_events(s, h):
        g = 2 * s + h
        src, dst = part.at[s], y.at[s]
        size = [None] + [strip >> j for j in range(bits)]
        start = [None, value[0] * (rows // 2) + h * strip]
        for j in range(1, bits):
            start.append(start[-1] + value[j] * size[j + 1])

        def away(j):
            if j == 0:
                return (1 - value[0]) * (rows // 2) + h * strip
            return start[j] + (1 - value[j]) * size[j + 1]

        def rs(j):
            return remote(src.at[span(away(j), size[j + 1]), :], rs_buf[j].at[g],
                          rs_s.at[g, j], rs_r.at[g, j], {"row": partner[j]})

        def ag(j):
            mine = span(start[1], size[1]) if j == 0 else span(start[j + 1], size[j + 1])
            return remote(dst.at[mine, :], dst.at[mine, :],
                          ag_s.at[g, j], ag_r.at[g, j], {"row": partner[j]})

        def add(j):
            rs(j).wait()
            mine = size[j + 1]
            step = min(mine, 128)

            def body(i):
                here = span(start[j + 1] + i * step, step)
                there = span(i * step, step)
                total = src[here, :] + rs_buf[j][g, there, :]
                if j == bits - 1:
                    block = lax.div(c * rows + start[j + 1] + i * step, width)
                    dst[here, :] = -live(s, block) * total
                else:
                    src[here, :] = total
            loop(0, mine // step, body)

        def cut(copy, i):
            size_ = strip // 8
            here = span(away(0) + i * size_, size_)
            mine = span(start[1] + i * size_, size_)
            if copy is rs:
                remote(src.at[here, :], rs_buf[0].at[g, span(i * size_, size_), :],
                       rs_s.at[g, 0], rs_r.at[g, 0], {"row": partner[0]}).start()
            else:
                remote(dst.at[mine, :], dst.at[mine, :],
                       ag_s.at[g, 0], ag_r.at[g, 0], {"row": partner[0]}).start()

        def event(i):
            if i < bits:
                add(i - 1)
                rs(i).start()
            elif i == bits:
                add(bits - 1)
                ag(bits - 1).start()
            else:
                j = 2 * bits - i
                ag(j).wait()
                if j > 1:
                    ag(j - 1).start()
        return [[functools.partial(cut, f, i) for i in range(8)] for f in (rs, ag)] + [
            functools.partial(event, i) for i in range(1, 2 * bits + 1)]

    def share_start(u):
        start = value[0] * (rows // 2) + (u // per) * strip + (u % per) * sub
        for j in range(1, bits):
            start = start + value[j] * (strip >> j)
        return start

    source = lax.div(r * n_cols, n_rows)
    own_start = r * depth - source * rows

    def target(s, u, plane, to_plane, src, send):
        at = plane * rows + share_start(u)
        to = lax.div(at, depth)
        offset = at - to * depth
        here, recv = low.at[s, span(offset, sub), :], low_r.at[s, lax.div(offset, sub)]
        return to, here, recv, remote(src, here, send, recv, {"row": to, "col": to_plane})

    def share(s, u):
        return y.at[s, span(share_start(u), sub), :]

    def z_copy(s, u, d, way):
        sem = zl_s if way < 0 else zr_s
        return target(s, u, c, c + way * d, share(s, u), sem.at[s, u, d])[3]

    def z_all(s, u, way, act):
        for d in range(end, 0, -1):
            @pl.when((c >= d) if way < 0 else (c + d <= end))
            def _(d=d):
                act(z_copy(s, u, d, way))

    def z_send(s, u, way):
        z_all(s, u, way, lambda copy: copy.start())

    def low_wait(s, i):
        here = low.at[s, span(i * sub, sub), :]
        pltpu.make_async_copy(here, here, low_r.at[s, i]).wait()

    def low_copy(s, i):
        here = span(i * sub, sub)
        return pltpu.make_async_copy(low.at[s, here, :], low_out.at[s, here, :], o_sem.at[s, i])

    def places(u):
        h, k = u // per, u % per
        return [a * (rows // 2) + h * strip + p * piece + k * sub
                for a in range(depth // (rows // 2)) for p in range(strip // piece)]

    def from_y(s, h):
        @pl.when(c == source)
        def _():
            for u in range(h * per, (h + 1) * per):
                for offset in places(u):
                    pltpu.make_async_copy(
                        y.at[s, span(own_start + offset, sub), :],
                        low.at[s, span(offset, sub), :], low_r.at[s, offset // sub],
                    ).start()

    def consume(s, u):
        def one(offset):
            i = lax.div(offset, sub)
            low_wait(s, i)
            here = span(offset, sub)
            low_copy(s, i).start()
            dpart[s] += dot3((bh[s, here, :], bl[s, here, :]), halves(low[s, here, :]),
                             (((0,), (0,)), ((), ())))
        for offset in places(u):
            one(offset)

    ds = width // n_rows

    def other(i):
        return lax.rem(r + i, n_rows)

    def da_copy(s, i, p):
        return remote(dpart.at[s, span(p * ds, ds), :], dbuf.at[s, i],
                      da_s.at[s, p], da_r.at[s, i], {"row": p})

    def db_copy(s, i, p):
        here = dsum.at[s, span(i * ds, ds), :]
        return remote(here, here, db_s.at[s, p], db_r.at[s, i], {"row": p})

    def diag_a(s):
        loop(1, n_rows, lambda i: da_copy(s, r, other(i)).start())

    def diag_b(s):
        mine = span(r * ds, ds)
        dsum[s, mine, :] = dpart[s, mine, :]

        def body(i):
            da_copy(s, other(i), other(i)).wait_recv()
            dsum[s, mine, :] += dbuf[s, other(i)]
        loop(1, n_rows, body)
        loop(1, n_rows, lambda i: db_copy(s, r, other(i)).start())

    def diag_c(s):
        loop(1, n_rows, lambda i: db_copy(s, other(i), other(i)).wait_recv())
        diag_out[s] = dsum[s]

    tb = rows // 8

    def turn_copy(i):
        s, b = i // 8, i % 8
        return pltpu.make_async_copy(
            turned.at[b], y_out.at[s, :, pl.ds(b * tb, tb)], t_sem.at[b]
        )

    def turn(i):
        s, b = i // 8, i % 8
        if s > 0:
            turn_copy(i - 8).wait()
        turned[b] = y[s, pl.ds(b * tb, tb), :].T
        turn_copy(i).start()

    events = []

    def at(time, f, *args):
        events.append((time, len(events), functools.partial(f, *args)))

    full = 2 * n_ch
    for s in range(2):
        b = n_ch * (s + 1)
        for h in range(2):
            out, back, *steps = reduce_events(s, h)
            when = [b + 5 + 4 * h] if s == 0 else [b + 4 + 2 * h]
            when += [b + 11 + 5 * (j - 2) + 4 * h for j in range(2, bits + 1)]
            last = when[-1]
            when += [last + 5 + 6 * j for j in range(bits)]
            for n, f in enumerate(out):
                at(b - 1 + 4 * h + n // 2 if s == 0 else b - 1 + 2 * h, f)
            for n, f in enumerate(back):
                at(when[-2] + (n // 2 if s == 0 else 0) + 0.25, f)
            for time, f in zip(when, steps):
                at(time, f)
            for u in range(h * per, (h + 1) * per):
                at(last + (4 if s == 0 else 0), z_send, s, u, 1)
                at(max(full - 1, last), z_send, s, u, -1)
            at(when[-1], from_y, s, h)
        done = when[-1]
        for i in range(8):
            at(max(full + (25.5 if s == 0 else 0), done + 0.5) + i / 8, turn, 8 * s + i)
        final = max(full + 28, done) if s == 0 else full + 50
        for u in range(n_sub):
            at(final + u / n_sub, consume, s, u)
        at(final + 1, diag_a, s)
        at(full + (49 if s == 0 else 52), diag_b, s)
        at(full + 53, diag_c, s)
    events.sort(key=lambda e: e[:2])

    barrier = pltpu.get_barrier_semaphore()
    loop(1, n_rows, lambda i: pl.semaphore_signal(
        barrier, inc=1, device_id={"row": other(i)}, device_id_type=MESH))

    @pl.when(c > 0)
    def _():
        pl.semaphore_signal(barrier, inc=1, device_id=left, device_id_type=MESH)

    @pl.when(c < end)
    def _():
        pl.semaphore_signal(barrier, inc=1, device_id=right, device_id_type=MESH)

    for m in range(ABUF - 1):
        a_copy(m).start()
    dpart[...] = jnp.zeros_like(dpart)

    def clear(i):
        for s in range(2):
            part[s, span(i * strip // 4, strip // 4), :] = jnp.zeros((strip // 4, width), F32)
    loop(0, 16, clear)

    beside = lax.div(c + end - 1, end) + lax.div(2 * end - 1 - c, end)
    pl.semaphore_wait(barrier, n_rows - 1 + beside)

    stop = 2 * n_ch + LAG
    inside = [e for e in events if e[0] < stop]
    outside = [e for e in events if e[0] >= stop]
    times = sorted({e[0] for e in inside})

    def body(u):
        up = u + AHEAD * (end - 2 * c)

        @pl.when((up >= 0) & (up < n_ch))
        def _():
            plus_step(up)

        @pl.when((u >= 0) & (u < n_ch))
        def _():
            lead_step(u)

        @pl.when((u >= n_ch) & (u < 2 * n_ch))
        def _():
            minus_step(u - n_ch)

        @pl.when((u >= LAG) & (u < 2 * n_ch + LAG))
        def _():
            multiply(u - LAG)

        for time in times:
            @pl.when(u == int(time))
            def _(time=time):
                for e in inside:
                    if e[0] == time:
                        e[2]()
    loop(-AHEAD * (end - c), stop, body)
    for e in outside:
        e[2]()

    def drain_panel(k):
        @pl.when(c > 0)
        def _():
            lead_copy(k).wait_send()

        @pl.when((c > 0) & (c < end))
        def _():
            minus_copy(k).wait_send()

        @pl.when(c < end)
        def _():
            plus_copy(k).wait_send()
    loop(0, n_ch, drain_panel)

    for s in range(2):
        for u in range(n_sub):
            for way in (-1, 1):
                z_all(s, u, way, lambda copy: copy.wait_send())
        loop(1, n_rows, lambda i: da_copy(s, r, other(i)).wait_send())
        loop(1, n_rows, lambda i: db_copy(s, r, other(i)).wait_send())
        loop(0, depth // sub, lambda i: low_copy(s, i).wait())
    for i in range(8, 16):
        turn_copy(i).wait()


def exchange(n_rows, n_cols, a, panel, pattern, slots):
    rows, depth = a.shape
    width = panel.shape[1]
    bits = n_rows.bit_length() - 1
    vmem = pl.BlockSpec(memory_space=pltpu.VMEM)
    smem = pl.BlockSpec(memory_space=pltpu.SMEM)
    anywhere = pl.BlockSpec(memory_space=pl.ANY)
    dma = pltpu.SemaphoreType.DMA
    kc = min(256, depth)
    n = depth // (kc // 4)
    strip = rows // 4
    piece = strip >> (bits - 1)
    sub = min(piece, 128)
    n_sub = 2 * piece // sub
    return pl.pallas_call(
        functools.partial(kernel, n_rows, n_cols),
        out_shape=(
            jax.ShapeDtypeStruct((2, width, rows), F32),
            jax.ShapeDtypeStruct((2, depth, width), F32),
            jax.ShapeDtypeStruct((2, width, width), F32),
        ),
        in_specs=[anywhere, vmem, smem, smem],
        out_specs=(anywhere, anywhere, vmem),
        scratch_shapes=[
            pltpu.VMEM((2, depth, width), BF16),
            pltpu.VMEM((2, depth, width), BF16),
            pltpu.VMEM((depth, width), F32),
            pltpu.VMEM((depth, width), F32),
            pltpu.VMEM((depth, width), F32),
            pltpu.VMEM((2, rows, width), F32),
            pltpu.VMEM((2, rows, width), F32),
            pltpu.VMEM((2, depth, width), F32),
            pltpu.VMEM((ABUF, strip, kc), F32),
            pltpu.VMEM((8, width, rows // 8), F32),
            pltpu.VMEM((2, width, width), F32),
            pltpu.VMEM((2, n_rows, width // n_rows, width), F32),
            pltpu.VMEM((2, width, width), F32),
            *[pltpu.VMEM((4, strip >> j, width), F32) for j in range(bits)],
            dma((n,)), dma((n,)), dma((n,)), dma((n,)), dma((n,)), dma((n,)),
            dma((4, bits)), dma((4, bits)), dma((4, bits)), dma((4, bits)),
            dma((2, n_sub, n_cols)), dma((2, n_sub, n_cols)),
            dma((2, depth // sub)),
            dma((2, n_rows)), dma((2, n_rows)), dma((2, n_rows)), dma((2, n_rows)),
            dma((ABUF,)), dma((8,)), dma((2, depth // sub)),
        ],
        compiler_params=pltpu.CompilerParams(
            collective_id=0, has_side_effects=True, vmem_limit_bytes=66_000_000
        ),
    )(a, panel, pattern, slots)


def settle_kernel(
    end, slots, y_in, low_in, dsum, dinv, y_out, low_out, diag_out, y_buf, low_buf, in_sem, out_sem
):
    lead_at = jnp.where(slots[0] == end, 0, 1)
    moves = []
    for s, at in ((0, lead_at), (1, 1 - lead_at)):
        for src, buf, dst, parts in ((y_in, y_buf, y_out, 4), (low_in, low_buf, low_out, 2)):
            size = buf.shape[1] // parts
            for p in range(parts):
                here, n = pl.ds(p * size, size), len(moves)
                moves.append((
                    pltpu.make_async_copy(src.at[at, here, :], buf.at[s, here, :], in_sem.at[n]),
                    pltpu.make_async_copy(buf.at[s, here, :], dst.at[s, here, :], out_sem.at[n]),
                ))
    for load, _ in moves:
        load.start()
    diag_out[0] = dinv[0] - dsum[lead_at]
    diag_out[1] = dinv[1] - dsum[1 - lead_at]
    for load, store in moves:
        load.wait()
        store.start()
    for _, store in moves:
        store.wait()


def settle(n_cols, slots, y, low, dsum, dinv):
    vmem = pl.BlockSpec(memory_space=pltpu.VMEM)
    smem = pl.BlockSpec(memory_space=pltpu.SMEM)
    anywhere = pl.BlockSpec(memory_space=pl.ANY)
    return pl.pallas_call(
        functools.partial(settle_kernel, n_cols - 1),
        out_shape=tuple(jax.ShapeDtypeStruct(x.shape, F32) for x in (y, low, dinv)),
        in_specs=[smem, anywhere, anywhere, vmem, vmem],
        out_specs=(anywhere, anywhere, vmem),
        scratch_shapes=[
            pltpu.VMEM(y.shape, F32), pltpu.VMEM(low.shape, F32),
            pltpu.SemaphoreType.DMA((12,)), pltpu.SemaphoreType.DMA((12,)),
        ],
        compiler_params=pltpu.CompilerParams(vmem_limit_bytes=66_000_000),
    )(slots, y, low, dsum, dinv)


def shards(inverse_rows, panels, diag_inverse, pattern, owner_slot):
    n_rows, n_cols = lax.axis_size("row"), lax.axis_size("col")
    y, low, dsum = exchange(n_rows, n_cols, inverse_rows, panels[0], pattern, owner_slot)
    y, low, diag = settle(n_cols, owner_slot, y, low, dsum, diag_inverse)
    return low, y, diag


def solution(mesh):
    in_specs = (P("col", "row"), P("col", "row", None), P(), P(), P())
    out_specs = (P(None, "row", None), P(None, None, "col"), P())
    return jax.shard_map(shards, mesh=mesh, in_specs=in_specs, out_specs=out_specs, check_vma=False)
```

```python
import functools

import jax
import jax.numpy as jnp
from jax import lax
from jax.experimental import pallas as pl
from jax.experimental.pallas import tpu as pltpu
from jax.sharding import PartitionSpec as P

MESH = pl.DeviceIdType.MESH
F32 = jnp.float32
BF16 = jnp.bfloat16
AHEAD = 3
LAG = 3
ABUF = 4


def halves(x):
    high = x.astype(BF16)
    return high, (x - high.astype(F32)).astype(BF16)


def dot3(a, b, dims=(((1,), (0,)), ((), ()))):
    (ah, al), (bh, bl) = a, b
    dot = functools.partial(lax.dot_general, dimension_numbers=dims, preferred_element_type=F32)
    return dot(ah, bh) + dot(ah, bl) + dot(al, bh)


def kernel(
    n_rows, n_cols,
    a_ref, panel, pattern_ref, slot_ref,
    y_out, low_out, diag_out,
    bh, bl, lead, plus, minus, part, y, low, abuf, turned, dpart, dbuf, dsum, *rest,
):
    bits = n_rows.bit_length() - 1
    rs_buf = rest[:bits]
    (lead_s, lead_r, plus_s, plus_r, minus_s, minus_r, rs_s, rs_r, ag_s, ag_r,
     zl_s, zr_s, low_r, da_s, da_r, db_s, db_r, a_sem, t_sem, o_sem) = rest[bits:]
    r = lax.axis_index("row")
    c = lax.axis_index("col")
    width = bh.shape[2]
    depth = bh.shape[1]
    rows = y.shape[1]
    end = n_cols - 1
    core = lax.rem(r, 2)
    left, right = {"col": c - 1}, {"col": c + 1}
    strip = rows // 4
    kc = abuf.shape[2]
    ch = kc // 4
    n_ch = depth // ch
    piece = strip >> (bits - 1)
    sub = min(piece, 128)
    per = piece // sub
    n_sub = 2 * per

    def bit_of(j):
        if j == 0:
            return 1
        return (1 << j) + core * ((1 << (bits - j)) - (1 << j))

    value = [lax.rem(lax.div(r, bit_of(j)), 2) for j in range(bits)]
    partner = [r + (1 - 2 * value[j]) * bit_of(j) for j in range(bits)]

    def span(start, size):
        return pl.ds(pl.multiple_of(start, 8), size)

    def chunk(k):
        return span(k * ch, ch)

    def remote(src, dst, send, recv, where):
        return pltpu.make_async_remote_copy(
            src_ref=src, dst_ref=dst, send_sem=send, recv_sem=recv,
            device_id=where, device_id_type=MESH,
        )

    def loop(low_, high_, body):
        def step(i, carry):
            body(i)
            return carry
        lax.fori_loop(low_, high_, step, 0)

    def lead_copy(k):
        ref = lead.at[chunk(k), :]
        return remote(ref, ref, lead_s.at[k], lead_r.at[k], left)

    def plus_copy(k):
        ref = plus.at[chunk(k), :]
        return remote(ref, ref, plus_s.at[k], plus_r.at[k], right)

    def minus_copy(k):
        ref = minus.at[chunk(k), :]
        return remote(ref, ref, minus_s.at[k], minus_r.at[k], left)

    lead_at = jnp.where(slot_ref[0] == end, 0, 1)

    def live(s, block):
        at_ = lead_at if s == 0 else 1 - lead_at
        return pattern_ref[at_, block].astype(F32)

    def own(s, k):
        block = lax.div(r * depth + k * ch, width)
        at_ = lead_at if s == 0 else 1 - lead_at
        here = jnp.where(slot_ref[at_] == c, 1.0, 0.0)
        return (live(s, block) * here) * panel[chunk(k), :]

    def keep(s, k, x):
        high, rest_ = halves(x)
        bh[s, chunk(k), :] = high
        bl[s, chunk(k), :] = rest_

    def plus_step(k):
        @pl.when(c > 0)
        def _():
            plus_copy(k).wait_recv()
            plus[chunk(k), :] = plus[chunk(k), :] + own(1, k)

        @pl.when(c == 0)
        def _():
            plus[chunk(k), :] = own(1, k)

        @pl.when(c < end)
        def _():
            plus_copy(k).start()

    def lead_step(k):
        @pl.when(c < end)
        def _():
            lead_copy(k).wait_recv()

        @pl.when(c == end)
        def _():
            lead[chunk(k), :] = own(0, k)

        @pl.when(c > 0)
        def _():
            lead_copy(k).start()
        keep(0, k, lead[chunk(k), :])

    def minus_step(k):
        @pl.when(c < end - 1)
        def _():
            minus_copy(k).wait_recv()
            minus[chunk(k), :] = minus[chunk(k), :] + own(1, k)

        @pl.when(c == end - 1)
        def _():
            minus[chunk(k), :] = own(1, k)

        @pl.when((c > 0) & (c < end))
        def _():
            minus_copy(k).start()

        @pl.when(c < end)
        def _():
            keep(1, k, (plus[chunk(k), :] + minus[chunk(k), :]) - own(1, k))

        @pl.when(c == end)
        def _():
            keep(1, k, plus[chunk(k), :])

    def quarter_start(q):
        half = (1 - value[0]) + lax.rem(q, 2) * (2 * value[0] - 1)
        return half * (rows // 2) + lax.div(q, 2) * strip

    def a_copy(m):
        k = lax.div(lax.rem(m, n_ch), 4)
        slot = lax.rem(m, ABUF)
        return pltpu.make_async_copy(
            a_ref.at[span(quarter_start(lax.rem(m, 4)), strip),
                     pl.ds(pl.multiple_of(k * kc, 128), kc)],
            abuf.at[slot], a_sem.at[slot],
        )

    tall = min(strip, 1024)

    def multiply(m):
        @pl.when(m + ABUF - 1 < 2 * n_ch)
        def _():
            a_copy(m + ABUF - 1).start()

        a_copy(m).wait()
        s = lax.div(m, n_ch)
        k = lax.div(lax.rem(m, n_ch), 4)
        slot = lax.rem(m, ABUF)
        start = quarter_start(lax.rem(m, 4))
        deep = pl.ds(pl.multiple_of(k * kc, 16), kc)

        @pl.when(k == 0)
        def _():
            part[s, span(start, strip), :] = jnp.zeros((strip, width), F32)

        def body(i):
            a = halves(abuf[slot, span(i * tall, tall), :])
            here = span(start + i * tall, tall)
            part[s, here, :] = part[s, here, :] + dot3(a, (bh[s, deep, :], bl[s, deep, :]))
        loop(0, strip // tall, body)

    def reduce_events(s, h):
        g = 2 * s + h
        src, dst = part.at[s], y.at[s]
        size = [None] + [strip >> j for j in range(bits)]
        start = [None, value[0] * (rows // 2) + h * strip]
        for j in range(1, bits):
            start.append(start[-1] + value[j] * size[j + 1])

        def away(j):
            if j == 0:
                return (1 - value[0]) * (rows // 2) + h * strip
            return start[j] + (1 - value[j]) * size[j + 1]

        def rs(j):
            return remote(src.at[span(away(j), size[j + 1]), :], rs_buf[j].at[g],
                          rs_s.at[g, j], rs_r.at[g, j], {"row": partner[j]})

        def ag(j):
            mine = span(start[1], size[1]) if j == 0 else span(start[j + 1], size[j + 1])
            return remote(dst.at[mine, :], dst.at[mine, :],
                          ag_s.at[g, j], ag_r.at[g, j], {"row": partner[j]})

        def add(j):
            rs(j).wait()
            mine = size[j + 1]
            step = min(mine, 128)

            def body(i):
                here = span(start[j + 1] + i * step, step)
                there = span(i * step, step)
                total = src[here, :] + rs_buf[j][g, there, :]
                if j == bits - 1:
                    block = lax.div(c * rows + start[j + 1] + i * step, width)
                    dst[here, :] = -live(s, block) * total
                else:
                    src[here, :] = total
            loop(0, mine // step, body)

        def cut(copy, i):
            size_ = strip // 8
            here = span(away(0) + i * size_, size_)
            mine = span(start[1] + i * size_, size_)
            if copy is rs:
                remote(src.at[here, :], rs_buf[0].at[g, span(i * size_, size_), :],
                       rs_s.at[g, 0], rs_r.at[g, 0], {"row": partner[0]}).start()
            else:
                remote(dst.at[mine, :], dst.at[mine, :],
                       ag_s.at[g, 0], ag_r.at[g, 0], {"row": partner[0]}).start()

        def event(i):
            if i < bits:
                add(i - 1)
                rs(i).start()
            elif i == bits:
                add(bits - 1)
                ag(bits - 1).start()
            else:
                j = 2 * bits - i
                ag(j).wait()
                if j > 1:
                    ag(j - 1).start()
        return [[functools.partial(cut, f, i) for i in range(8)] for f in (rs, ag)] + [
            functools.partial(event, i) for i in range(1, 2 * bits + 1)]

    def share_start(u):
        start = value[0] * (rows // 2) + (u // per) * strip + (u % per) * sub
        for j in range(1, bits):
            start = start + value[j] * (strip >> j)
        return start

    source = lax.div(r * n_cols, n_rows)
    own_start = r * depth - source * rows

    def target(s, u, plane, to_plane, src, send):
        at = plane * rows + share_start(u)
        to = lax.div(at, depth)
        offset = at - to * depth
        here, recv = low.at[s, span(offset, sub), :], low_r.at[s, lax.div(offset, sub)]
        return to, here, recv, remote(src, here, send, recv, {"row": to, "col": to_plane})

    def share(s, u):
        return y.at[s, span(share_start(u), sub), :]

    def z_copy(s, u, d, way):
        sem = zl_s if way < 0 else zr_s
        return target(s, u, c, c + way * d, share(s, u), sem.at[s, u, d])[3]

    def z_all(s, u, way, act):
        for d in range(end, 0, -1):
            @pl.when((c >= d) if way < 0 else (c + d <= end))
            def _(d=d):
                act(z_copy(s, u, d, way))

    def z_send(s, u, way):
        z_all(s, u, way, lambda copy: copy.start())

    def low_wait(s, i):
        here = low.at[s, span(i * sub, sub), :]
        pltpu.make_async_copy(here, here, low_r.at[s, i]).wait()

    def low_copy(s, i):
        here = span(i * sub, sub)
        return pltpu.make_async_copy(low.at[s, here, :], low_out.at[s, here, :], o_sem.at[s, i])

    def places(u):
        h, k = u // per, u % per
        return [a * (rows // 2) + h * strip + p * piece + k * sub
                for a in range(depth // (rows // 2)) for p in range(strip // piece)]

    def from_y(s, h):
        @pl.when(c == source)
        def _():
            for u in range(h * per, (h + 1) * per):
                for offset in places(u):
                    pltpu.make_async_copy(
                        y.at[s, span(own_start + offset, sub), :],
                        low.at[s, span(offset, sub), :], low_r.at[s, offset // sub],
                    ).start()

    def consume(s, u):
        def one(offset):
            i = lax.div(offset, sub)
            low_wait(s, i)
            here = span(offset, sub)
            low_copy(s, i).start()
            dpart[s] += dot3((bh[s, here, :], bl[s, here, :]), halves(low[s, here, :]),
                             (((0,), (0,)), ((), ())))
        for offset in places(u):
            one(offset)

    ds = width // n_rows

    def other(i):
        return lax.rem(r + i, n_rows)

    def da_copy(s, i, p):
        return remote(dpart.at[s, span(p * ds, ds), :], dbuf.at[s, i],
                      da_s.at[s, p], da_r.at[s, i], {"row": p})

    def db_copy(s, i, p):
        here = dsum.at[s, span(i * ds, ds), :]
        return remote(here, here, db_s.at[s, p], db_r.at[s, i], {"row": p})

    def diag_a(s):
        loop(1, n_rows, lambda i: da_copy(s, r, other(i)).start())

    def diag_b(s):
        mine = span(r * ds, ds)
        dsum[s, mine, :] = dpart[s, mine, :]

        def body(i):
            da_copy(s, other(i), other(i)).wait_recv()
            dsum[s, mine, :] += dbuf[s, other(i)]
        loop(1, n_rows, body)
        loop(1, n_rows, lambda i: db_copy(s, r, other(i)).start())

    def diag_c(s):
        loop(1, n_rows, lambda i: db_copy(s, other(i), other(i)).wait_recv())
        diag_out[s] = dsum[s]

    tb = rows // 8

    def turn_copy(i):
        s, b = i // 8, i % 8
        return pltpu.make_async_copy(
            turned.at[b], y_out.at[s, :, pl.ds(b * tb, tb)], t_sem.at[b]
        )

    def turn(i):
        s, b = i // 8, i % 8
        if s > 0:
            turn_copy(i - 8).wait()
        turned[b] = y[s, pl.ds(b * tb, tb), :].T
        turn_copy(i).start()

    events = []

    def at(time, f, *args):
        events.append((time, len(events), functools.partial(f, *args)))

    full = 2 * n_ch
    for s in range(2):
        b = n_ch * (s + 1)
        for h in range(2):
            out, back, *steps = reduce_events(s, h)
            when = [b + 5 + 4 * h] if s == 0 else [b + 4 + 2 * h]
            when += [b + 11 + 5 * (j - 2) + 4 * h for j in range(2, bits + 1)]
            last = when[-1]
            when += [last + 5 + 6 * j for j in range(bits)]
            for n, f in enumerate(out):
                at(b - 1 + 4 * h + n // 2 if s == 0 else b - 1 + 2 * h, f)
            for n, f in enumerate(back):
                at(when[-2] + (n // 2 if s == 0 else 0) + 0.25, f)
            for time, f in zip(when, steps):
                at(time, f)
            for u in range(h * per, (h + 1) * per):
                at(last + (4 if s == 0 else 0), z_send, s, u, 1)
                at(max(full - 1, last), z_send, s, u, -1)
            at(when[-1], from_y, s, h)
        done = when[-1]
        for i in range(8):
            at(max(full + (25.5 if s == 0 else 0), done + 0.5) + i / 8, turn, 8 * s + i)
        final = max(full + 28, done) if s == 0 else full + 50
        for u in range(n_sub):
            at(final + u / n_sub, consume, s, u)
        at(final + 1, diag_a, s)
        at(full + (49 if s == 0 else 52), diag_b, s)
        at(full + 53, diag_c, s)
    events.sort(key=lambda e: e[:2])

    barrier = pltpu.get_barrier_semaphore()
    loop(1, n_rows, lambda i: pl.semaphore_signal(
        barrier, inc=1, device_id={"row": other(i)}, device_id_type=MESH))

    @pl.when(c > 0)
    def _():
        pl.semaphore_signal(barrier, inc=1, device_id=left, device_id_type=MESH)

    @pl.when(c < end)
    def _():
        pl.semaphore_signal(barrier, inc=1, device_id=right, device_id_type=MESH)

    for m in range(ABUF - 1):
        a_copy(m).start()
    dpart[...] = jnp.zeros_like(dpart)

    beside = lax.div(c + end - 1, end) + lax.div(2 * end - 1 - c, end)
    pl.semaphore_wait(barrier, n_rows - 1 + beside)

    stop = 2 * n_ch + LAG
    inside = [e for e in events if e[0] < stop]
    outside = [e for e in events if e[0] >= stop]
    times = sorted({e[0] for e in inside})

    def body(u):
        up = u + AHEAD * (end - 2 * c)

        @pl.when((up >= 0) & (up < n_ch))
        def _():
            plus_step(up)

        @pl.when((u >= 0) & (u < n_ch))
        def _():
            lead_step(u)

        @pl.when((u >= n_ch) & (u < 2 * n_ch))
        def _():
            minus_step(u - n_ch)

        @pl.when((u >= LAG) & (u < 2 * n_ch + LAG))
        def _():
            multiply(u - LAG)

        for time in times:
            @pl.when(u == int(time))
            def _(time=time):
                for e in inside:
                    if e[0] == time:
                        e[2]()
    loop(-AHEAD * (end - c), stop, body)
    for e in outside:
        e[2]()

    def drain_panel(k):
        @pl.when(c > 0)
        def _():
            lead_copy(k).wait_send()

        @pl.when((c > 0) & (c < end))
        def _():
            minus_copy(k).wait_send()

        @pl.when(c < end)
        def _():
            plus_copy(k).wait_send()
    loop(0, n_ch, drain_panel)

    for s in range(2):
        for u in range(n_sub):
            for way in (-1, 1):
                z_all(s, u, way, lambda copy: copy.wait_send())
        loop(1, n_rows, lambda i: da_copy(s, r, other(i)).wait_send())
        loop(1, n_rows, lambda i: db_copy(s, r, other(i)).wait_send())
        loop(0, depth // sub, lambda i: low_copy(s, i).wait())
    for i in range(8, 16):
        turn_copy(i).wait()


def exchange(n_rows, n_cols, a, panel, pattern, slots):
    rows, depth = a.shape
    width = panel.shape[1]
    bits = n_rows.bit_length() - 1
    vmem = pl.BlockSpec(memory_space=pltpu.VMEM)
    smem = pl.BlockSpec(memory_space=pltpu.SMEM)
    anywhere = pl.BlockSpec(memory_space=pl.ANY)
    dma = pltpu.SemaphoreType.DMA
    kc = min(256, depth)
    n = depth // (kc // 4)
    strip = rows // 4
    piece = strip >> (bits - 1)
    sub = min(piece, 128)
    n_sub = 2 * piece // sub
    return pl.pallas_call(
        functools.partial(kernel, n_rows, n_cols),
        out_shape=(
            jax.ShapeDtypeStruct((2, width, rows), F32),
            jax.ShapeDtypeStruct((2, depth, width), F32),
            jax.ShapeDtypeStruct((2, width, width), F32),
        ),
        in_specs=[anywhere, vmem, smem, smem],
        out_specs=(anywhere, anywhere, vmem),
        scratch_shapes=[
            pltpu.VMEM((2, depth, width), BF16),
            pltpu.VMEM((2, depth, width), BF16),
            pltpu.VMEM((depth, width), F32),
            pltpu.VMEM((depth, width), F32),
            pltpu.VMEM((depth, width), F32),
            pltpu.VMEM((2, rows, width), F32),
            pltpu.VMEM((2, rows, width), F32),
            pltpu.VMEM((2, depth, width), F32),
            pltpu.VMEM((ABUF, strip, kc), F32),
            pltpu.VMEM((8, width, rows // 8), F32),
            pltpu.VMEM((2, width, width), F32),
            pltpu.VMEM((2, n_rows, width // n_rows, width), F32),
            pltpu.VMEM((2, width, width), F32),
            *[pltpu.VMEM((4, strip >> j, width), F32) for j in range(bits)],
            dma((n,)), dma((n,)), dma((n,)), dma((n,)), dma((n,)), dma((n,)),
            dma((4, bits)), dma((4, bits)), dma((4, bits)), dma((4, bits)),
            dma((2, n_sub, n_cols)), dma((2, n_sub, n_cols)),
            dma((2, depth // sub)),
            dma((2, n_rows)), dma((2, n_rows)), dma((2, n_rows)), dma((2, n_rows)),
            dma((ABUF,)), dma((8,)), dma((2, depth // sub)),
        ],
        compiler_params=pltpu.CompilerParams(
            collective_id=0, has_side_effects=True, vmem_limit_bytes=66_000_000
        ),
    )(a, panel, pattern, slots)


def settle_kernel(
    end, slots, y_in, low_in, dsum, dinv, y_out, low_out, diag_out, y_buf, low_buf, in_sem, out_sem
):
    lead_at = jnp.where(slots[0] == end, 0, 1)
    moves = []
    for s, at in ((0, lead_at), (1, 1 - lead_at)):
        for src, buf, dst, parts in ((y_in, y_buf, y_out, 4), (low_in, low_buf, low_out, 2)):
            size = buf.shape[1] // parts
            for p in range(parts):
                here, n = pl.ds(p * size, size), len(moves)
                moves.append((
                    pltpu.make_async_copy(src.at[at, here, :], buf.at[s, here, :], in_sem.at[n]),
                    pltpu.make_async_copy(buf.at[s, here, :], dst.at[s, here, :], out_sem.at[n]),
                ))
    for load, _ in moves:
        load.start()
    diag_out[0] = dinv[0] - dsum[lead_at]
    diag_out[1] = dinv[1] - dsum[1 - lead_at]
    for load, store in moves:
        load.wait()
        store.start()
    for _, store in moves:
        store.wait()


def settle(n_cols, slots, y, low, dsum, dinv):
    vmem = pl.BlockSpec(memory_space=pltpu.VMEM)
    smem = pl.BlockSpec(memory_space=pltpu.SMEM)
    anywhere = pl.BlockSpec(memory_space=pl.ANY)
    return pl.pallas_call(
        functools.partial(settle_kernel, n_cols - 1),
        out_shape=tuple(jax.ShapeDtypeStruct(x.shape, F32) for x in (y, low, dinv)),
        in_specs=[smem, anywhere, anywhere, vmem, vmem],
        out_specs=(anywhere, anywhere, vmem),
        scratch_shapes=[
            pltpu.VMEM(y.shape, F32), pltpu.VMEM(low.shape, F32),
            pltpu.SemaphoreType.DMA((12,)), pltpu.SemaphoreType.DMA((12,)),
        ],
        compiler_params=pltpu.CompilerParams(vmem_limit_bytes=66_000_000),
    )(slots, y, low, dsum, dinv)


def shards(inverse_rows, panels, diag_inverse, pattern, owner_slot):
    n_rows, n_cols = lax.axis_size("row"), lax.axis_size("col")
    y, low, dsum = exchange(n_rows, n_cols, inverse_rows, panels[0], pattern, owner_slot)
    y, low, diag = settle(n_cols, owner_slot, y, low, dsum, diag_inverse)
    return low, y, diag


def solution(mesh):
    in_specs = (P("col", "row"), P("col", "row", None), P(), P(), P())
    out_specs = (P(None, "row", None), P(None, None, "col"), P())
    return jax.shard_map(shards, mesh=mesh, in_specs=in_specs, out_specs=out_specs, check_vma=False)
```

```python
import functools

import jax
import jax.numpy as jnp
from jax import lax
from jax.experimental import pallas as pl
from jax.experimental.pallas import tpu as pltpu
from jax.sharding import PartitionSpec as P

MESH = pl.DeviceIdType.MESH
F32 = jnp.float32
BF16 = jnp.bfloat16
AHEAD = 3
LAG = 3
ABUF = 4


def halves(x):
    high = x.astype(BF16)
    return high, (x - high.astype(F32)).astype(BF16)


def dot3(a, b, dims=(((1,), (0,)), ((), ()))):
    (ah, al), (bh, bl) = a, b
    dot = functools.partial(lax.dot_general, dimension_numbers=dims, preferred_element_type=F32)
    return dot(ah, bh) + dot(ah, bl) + dot(al, bh)


def kernel(
    n_rows, n_cols,
    a_ref, panel, pattern_ref, slot_ref,
    y_out, low_out, diag_out,
    bh, bl, lead, plus, minus, part, y, low, abuf, turned, dpart, dbuf, dsum, *rest,
):
    bits = n_rows.bit_length() - 1
    rs_buf = rest[:bits]
    (lead_s, lead_r, plus_s, plus_r, minus_s, minus_r, rs_s, rs_r, ag_s, ag_r,
     zl_s, zr_s, low_r, da_s, da_r, db_s, db_r, a_sem, t_sem, o_sem) = rest[bits:]
    r = lax.axis_index("row")
    c = lax.axis_index("col")
    width = bh.shape[2]
    depth = bh.shape[1]
    rows = y.shape[1]
    end = n_cols - 1
    core = lax.rem(r, 2)
    left, right = {"col": c - 1}, {"col": c + 1}
    strip = rows // 4
    kc = abuf.shape[2]
    ch = kc // 4
    n_ch = depth // ch
    piece = strip >> (bits - 1)
    sub = min(piece, 128)
    per = piece // sub
    n_sub = 2 * per

    def bit_of(j):
        if j == 0:
            return 1
        return (1 << j) + core * ((1 << (bits - j)) - (1 << j))

    value = [lax.rem(lax.div(r, bit_of(j)), 2) for j in range(bits)]
    partner = [r + (1 - 2 * value[j]) * bit_of(j) for j in range(bits)]

    def span(start, size):
        return pl.ds(pl.multiple_of(start, 8), size)

    def chunk(k):
        return span(k * ch, ch)

    def remote(src, dst, send, recv, where):
        return pltpu.make_async_remote_copy(
            src_ref=src, dst_ref=dst, send_sem=send, recv_sem=recv,
            device_id=where, device_id_type=MESH,
        )

    def loop(low_, high_, body):
        def step(i, carry):
            body(i)
            return carry
        lax.fori_loop(low_, high_, step, 0)

    def lead_copy(k):
        ref = lead.at[chunk(k), :]
        return remote(ref, ref, lead_s.at[k], lead_r.at[k], left)

    def plus_copy(k):
        ref = plus.at[chunk(k), :]
        return remote(ref, ref, plus_s.at[k], plus_r.at[k], right)

    def minus_copy(k):
        ref = minus.at[chunk(k), :]
        return remote(ref, ref, minus_s.at[k], minus_r.at[k], left)

    lead_at = jnp.where(slot_ref[0] == end, 0, 1)

    def live(s, block):
        at_ = lead_at if s == 0 else 1 - lead_at
        return pattern_ref[at_, block].astype(F32)

    def own(s, k):
        block = lax.div(r * depth + k * ch, width)
        at_ = lead_at if s == 0 else 1 - lead_at
        here = jnp.where(slot_ref[at_] == c, 1.0, 0.0)
        return (live(s, block) * here) * panel[chunk(k), :]

    def keep(s, k, x):
        high, rest_ = halves(x)
        bh[s, chunk(k), :] = high
        bl[s, chunk(k), :] = rest_

    def plus_step(k):
        @pl.when(c > 0)
        def _():
            plus_copy(k).wait_recv()
            plus[chunk(k), :] = plus[chunk(k), :] + own(1, k)

        @pl.when(c == 0)
        def _():
            plus[chunk(k), :] = own(1, k)

        @pl.when(c < end)
        def _():
            plus_copy(k).start()

    def lead_step(k):
        @pl.when(c < end)
        def _():
            lead_copy(k).wait_recv()

        @pl.when(c == end)
        def _():
            lead[chunk(k), :] = own(0, k)

        @pl.when(c > 0)
        def _():
            lead_copy(k).start()
        keep(0, k, lead[chunk(k), :])

    def minus_step(k):
        @pl.when(c < end - 1)
        def _():
            minus_copy(k).wait_recv()
            minus[chunk(k), :] = minus[chunk(k), :] + own(1, k)

        @pl.when(c == end - 1)
        def _():
            minus[chunk(k), :] = own(1, k)

        @pl.when((c > 0) & (c < end))
        def _():
            minus_copy(k).start()

        @pl.when(c < end)
        def _():
            keep(1, k, (plus[chunk(k), :] + minus[chunk(k), :]) - own(1, k))

        @pl.when(c == end)
        def _():
            keep(1, k, plus[chunk(k), :])

    def quarter_start(q):
        half = (1 - value[0]) + lax.rem(q, 2) * (2 * value[0] - 1)
        return half * (rows // 2) + lax.div(q, 2) * strip

    def a_copy(m):
        k = lax.div(lax.rem(m, n_ch), 4)
        slot = lax.rem(m, ABUF)
        return pltpu.make_async_copy(
            a_ref.at[span(quarter_start(lax.rem(m, 4)), strip),
                     pl.ds(pl.multiple_of(k * kc, 128), kc)],
            abuf.at[slot], a_sem.at[slot],
        )

    tall = min(strip, 1024)

    def multiply(m):
        @pl.when(m + ABUF - 1 < 2 * n_ch)
        def _():
            a_copy(m + ABUF - 1).start()

        a_copy(m).wait()
        s = lax.div(m, n_ch)
        k = lax.div(lax.rem(m, n_ch), 4)
        slot = lax.rem(m, ABUF)
        start = quarter_start(lax.rem(m, 4))
        deep = pl.ds(pl.multiple_of(k * kc, 16), kc)

        def body(i):
            a = halves(abuf[slot, span(i * tall, tall), :])
            here = span(start + i * tall, tall)
            part[s, here, :] = part[s, here, :] + dot3(a, (bh[s, deep, :], bl[s, deep, :]))
        loop(0, strip // tall, body)

    def reduce_events(s, h):
        g = 2 * s + h
        src, dst = part.at[s], y.at[s]
        size = [None] + [strip >> j for j in range(bits)]
        start = [None, value[0] * (rows // 2) + h * strip]
        for j in range(1, bits):
            start.append(start[-1] + value[j] * size[j + 1])

        def away(j):
            if j == 0:
                return (1 - value[0]) * (rows // 2) + h * strip
            return start[j] + (1 - value[j]) * size[j + 1]

        def rs(j):
            return remote(src.at[span(away(j), size[j + 1]), :], rs_buf[j].at[g],
                          rs_s.at[g, j], rs_r.at[g, j], {"row": partner[j]})

        def ag(j):
            mine = span(start[1], size[1]) if j == 0 else span(start[j + 1], size[j + 1])
            return remote(dst.at[mine, :], dst.at[mine, :],
                          ag_s.at[g, j], ag_r.at[g, j], {"row": partner[j]})

        def add(j):
            rs(j).wait()
            mine = size[j + 1]
            step = min(mine, 128)

            def body(i):
                here = span(start[j + 1] + i * step, step)
                there = span(i * step, step)
                total = src[here, :] + rs_buf[j][g, there, :]
                if j == bits - 1:
                    block = lax.div(c * rows + start[j + 1] + i * step, width)
                    dst[here, :] = -live(s, block) * total
                else:
                    src[here, :] = total
            loop(0, mine // step, body)

        def cut(copy, i):
            size_ = strip // 8
            here = span(away(0) + i * size_, size_)
            mine = span(start[1] + i * size_, size_)
            if copy is rs:
                remote(src.at[here, :], rs_buf[0].at[g, span(i * size_, size_), :],
                       rs_s.at[g, 0], rs_r.at[g, 0], {"row": partner[0]}).start()
            else:
                remote(dst.at[mine, :], dst.at[mine, :],
                       ag_s.at[g, 0], ag_r.at[g, 0], {"row": partner[0]}).start()

        def event(i):
            if i < bits:
                add(i - 1)
                rs(i).start()
            elif i == bits:
                add(bits - 1)
                ag(bits - 1).start()
            else:
                j = 2 * bits - i
                ag(j).wait()
                if j > 1:
                    ag(j - 1).start()
        return [[functools.partial(cut, f, i) for i in range(8)] for f in (rs, ag)] + [
            functools.partial(event, i) for i in range(1, 2 * bits + 1)]

    def share_start(u):
        start = value[0] * (rows // 2) + (u // per) * strip + (u % per) * sub
        for j in range(1, bits):
            start = start + value[j] * (strip >> j)
        return start

    source = lax.div(r * n_cols, n_rows)
    own_start = r * depth - source * rows

    def target(s, u, plane, to_plane, src, send):
        at = plane * rows + share_start(u)
        to = lax.div(at, depth)
        offset = at - to * depth
        here, recv = low.at[s, span(offset, sub), :], low_r.at[s, lax.div(offset, sub)]
        return to, here, recv, remote(src, here, send, recv, {"row": to, "col": to_plane})

    def share(s, u):
        return y.at[s, span(share_start(u), sub), :]

    def z_copy(s, u, d, way):
        sem = zl_s if way < 0 else zr_s
        return target(s, u, c, c + way * d, share(s, u), sem.at[s, u, d])[3]

    def z_all(s, u, way, act):
        for d in range(end, 0, -1):
            @pl.when((c >= d) if way < 0 else (c + d <= end))
            def _(d=d):
                act(z_copy(s, u, d, way))

    def z_send(s, u, way):
        z_all(s, u, way, lambda copy: copy.start())

    def low_wait(s, i):
        here = low.at[s, span(i * sub, sub), :]
        pltpu.make_async_copy(here, here, low_r.at[s, i]).wait()

    def low_copy(s, i):
        here = span(i * sub, sub)
        return pltpu.make_async_copy(low.at[s, here, :], low_out.at[s, here, :], o_sem.at[s, i])

    def places(u):
        h, k = u // per, u % per
        return [a * (rows // 2) + h * strip + p * piece + k * sub
                for a in range(depth // (rows // 2)) for p in range(strip // piece)]

    def from_y(s, h):
        @pl.when(c == source)
        def _():
            for u in range(h * per, (h + 1) * per):
                for offset in places(u):
                    pltpu.make_async_copy(
                        y.at[s, span(own_start + offset, sub), :],
                        low.at[s, span(offset, sub), :], low_r.at[s, offset // sub],
                    ).start()

    def consume(s, u):
        def one(offset):
            i = lax.div(offset, sub)
            low_wait(s, i)
            here = span(offset, sub)
            low_copy(s, i).start()
            dpart[s] += dot3((bh[s, here, :], bl[s, here, :]), halves(low[s, here, :]),
                             (((0,), (0,)), ((), ())))
        for offset in places(u):
            one(offset)

    ds = width // n_rows

    def other(i):
        return lax.rem(r + i, n_rows)

    def da_copy(s, i, p):
        return remote(dpart.at[s, span(p * ds, ds), :], dbuf.at[s, i],
                      da_s.at[s, p], da_r.at[s, i], {"row": p})

    def db_copy(s, i, p):
        here = dsum.at[s, span(i * ds, ds), :]
        return remote(here, here, db_s.at[s, p], db_r.at[s, i], {"row": p})

    def diag_a(s):
        loop(1, n_rows, lambda i: da_copy(s, r, other(i)).start())

    def diag_b(s):
        mine = span(r * ds, ds)
        dsum[s, mine, :] = dpart[s, mine, :]

        def body(i):
            da_copy(s, other(i), other(i)).wait_recv()
            dsum[s, mine, :] += dbuf[s, other(i)]
        loop(1, n_rows, body)
        loop(1, n_rows, lambda i: db_copy(s, r, other(i)).start())

    def diag_c(s):
        loop(1, n_rows, lambda i: db_copy(s, other(i), other(i)).wait_recv())
        diag_out[s] = dsum[s]

    tb = rows // 8

    def turn_copy(i):
        s, b = i // 8, i % 8
        return pltpu.make_async_copy(
            turned.at[b], y_out.at[s, :, pl.ds(b * tb, tb)], t_sem.at[b]
        )

    def turn(i):
        s, b = i // 8, i % 8
        if s > 0:
            turn_copy(i - 8).wait()
        turned[b] = y[s, pl.ds(b * tb, tb), :].T
        turn_copy(i).start()

    events = []

    def at(time, f, *args):
        events.append((time, len(events), functools.partial(f, *args)))

    full = 2 * n_ch
    for s in range(2):
        b = n_ch * (s + 1)
        for h in range(2):
            out, back, *steps = reduce_events(s, h)
            when = [b + 5 + 4 * h] if s == 0 else [b + 4 + 2 * h]
            when += [b + 11 + 5 * (j - 2) + 4 * h for j in range(2, bits + 1)]
            last = when[-1]
            when += [last + 5 + 6 * j for j in range(bits)]
            for n, f in enumerate(out):
                at(b - 1 + 4 * h + n // 2 if s == 0 else b - 1 + 2 * h, f)
            for n, f in enumerate(back):
                at(when[-2] + (n // 2 if s == 0 else 0) + 0.25, f)
            for time, f in zip(when, steps):
                at(time, f)
            for u in range(h * per, (h + 1) * per):
                at(last + (4 if s == 0 else 0), z_send, s, u, 1)
                at(max(full - 1, last), z_send, s, u, -1)
            at(when[-1], from_y, s, h)
        done = when[-1]
        for i in range(8):
            at(max(full + (25.5 if s == 0 else 0), done + 0.5) + i / 8, turn, 8 * s + i)
        final = max(full + 28, done) if s == 0 else full + 50
        for u in range(n_sub):
            at(final + u / n_sub, consume, s, u)
        at(final + 1, diag_a, s)
        at(full + (49 if s == 0 else 52), diag_b, s)
        at(full + 53, diag_c, s)
    events.sort(key=lambda e: e[:2])

    barrier = pltpu.get_barrier_semaphore()
    loop(1, n_rows, lambda i: pl.semaphore_signal(
        barrier, inc=1, device_id={"row": other(i)}, device_id_type=MESH))

    @pl.when(c > 0)
    def _():
        pl.semaphore_signal(barrier, inc=1, device_id=left, device_id_type=MESH)

    @pl.when(c < end)
    def _():
        pl.semaphore_signal(barrier, inc=1, device_id=right, device_id_type=MESH)

    for m in range(ABUF - 1):
        a_copy(m).start()
    dpart[...] = jnp.zeros_like(dpart)

    def clear(i):
        for s in range(2):
            part[s, span(i * strip // 4, strip // 4), :] = jnp.zeros((strip // 4, width), F32)
    loop(0, 16, clear)

    beside = lax.div(c + end - 1, end) + lax.div(2 * end - 1 - c, end)
    pl.semaphore_wait(barrier, n_rows - 1 + beside)

    stop = 2 * n_ch + LAG
    inside = [e for e in events if e[0] < stop]
    outside = [e for e in events if e[0] >= stop]
    times = sorted({e[0] for e in inside})

    def body(u):
        up = u + AHEAD * (end - 2 * c)

        @pl.when((up >= 0) & (up < n_ch))
        def _():
            plus_step(up)

        @pl.when((u >= 0) & (u < n_ch))
        def _():
            lead_step(u)

        @pl.when((u >= n_ch) & (u < 2 * n_ch))
        def _():
            minus_step(u - n_ch)

        @pl.when((u >= LAG) & (u < 2 * n_ch + LAG))
        def _():
            multiply(u - LAG)

        for time in times:
            @pl.when(u == int(time))
            def _(time=time):
                for e in inside:
                    if e[0] == time:
                        e[2]()
    loop(-AHEAD * (end - c), stop, body)
    for e in outside:
        e[2]()

    def drain_panel(k):
        @pl.when(c > 0)
        def _():
            lead_copy(k).wait_send()

        @pl.when((c > 0) & (c < end))
        def _():
            minus_copy(k).wait_send()

        @pl.when(c < end)
        def _():
            plus_copy(k).wait_send()
    loop(0, n_ch, drain_panel)

    for s in range(2):
        for u in range(n_sub):
            for way in (-1, 1):
                z_all(s, u, way, lambda copy: copy.wait_send())
        loop(1, n_rows, lambda i: da_copy(s, r, other(i)).wait_send())
        loop(1, n_rows, lambda i: db_copy(s, r, other(i)).wait_send())
        loop(0, depth // sub, lambda i: low_copy(s, i).wait())
    for i in range(8, 16):
        turn_copy(i).wait()


def exchange(n_rows, n_cols, a, panel, pattern, slots):
    rows, depth = a.shape
    width = panel.shape[1]
    bits = n_rows.bit_length() - 1
    vmem = pl.BlockSpec(memory_space=pltpu.VMEM)
    smem = pl.BlockSpec(memory_space=pltpu.SMEM)
    anywhere = pl.BlockSpec(memory_space=pl.ANY)
    dma = pltpu.SemaphoreType.DMA
    kc = min(256, depth)
    n = depth // (kc // 4)
    strip = rows // 4
    piece = strip >> (bits - 1)
    sub = min(piece, 128)
    n_sub = 2 * piece // sub
    return pl.pallas_call(
        functools.partial(kernel, n_rows, n_cols),
        out_shape=(
            jax.ShapeDtypeStruct((2, width, rows), F32),
            jax.ShapeDtypeStruct((2, depth, width), F32),
            jax.ShapeDtypeStruct((2, width, width), F32),
        ),
        in_specs=[anywhere, vmem, smem, smem],
        out_specs=(anywhere, anywhere, vmem),
        scratch_shapes=[
            pltpu.VMEM((2, depth, width), BF16),
            pltpu.VMEM((2, depth, width), BF16),
            pltpu.VMEM((depth, width), F32),
            pltpu.VMEM((depth, width), F32),
            pltpu.VMEM((depth, width), F32),
            pltpu.VMEM((2, rows, width), F32),
            pltpu.VMEM((2, rows, width), F32),
            pltpu.VMEM((2, depth, width), F32),
            pltpu.VMEM((ABUF, strip, kc), F32),
            pltpu.VMEM((8, width, rows // 8), F32),
            pltpu.VMEM((2, width, width), F32),
            pltpu.VMEM((2, n_rows, width // n_rows, width), F32),
            pltpu.VMEM((2, width, width), F32),
            *[pltpu.VMEM((4, strip >> j, width), F32) for j in range(bits)],
            dma((n,)), dma((n,)), dma((n,)), dma((n,)), dma((n,)), dma((n,)),
            dma((4, bits)), dma((4, bits)), dma((4, bits)), dma((4, bits)),
            dma((2, n_sub, n_cols)), dma((2, n_sub, n_cols)),
            dma((2, depth // sub)),
            dma((2, n_rows)), dma((2, n_rows)), dma((2, n_rows)), dma((2, n_rows)),
            dma((ABUF,)), dma((8,)), dma((2, depth // sub)),
        ],
        compiler_params=pltpu.CompilerParams(
            collective_id=0, has_side_effects=True, vmem_limit_bytes=66_000_000
        ),
    )(a, panel, pattern, slots)


def settle_kernel(
    end, slots, y_in, low_in, dsum, dinv, y_out, low_out, diag_out, y_buf, low_buf, in_sem, out_sem
):
    lead_at = jnp.where(slots[0] == end, 0, 1)
    moves = []
    for s, at in ((0, lead_at), (1, 1 - lead_at)):
        for src, buf, dst, parts in ((y_in, y_buf, y_out, 8), (low_in, low_buf, low_out, 4)):
            size = buf.shape[1] // parts
            for p in range(parts):
                here, n = pl.ds(p * size, size), len(moves)
                moves.append((
                    pltpu.make_async_copy(src.at[at, here, :], buf.at[s, here, :], in_sem.at[n]),
                    pltpu.make_async_copy(buf.at[s, here, :], dst.at[s, here, :], out_sem.at[n]),
                ))
    for load, _ in moves:
        load.start()
    diag_out[0] = dinv[0] - dsum[lead_at]
    diag_out[1] = dinv[1] - dsum[1 - lead_at]
    for load, store in moves:
        load.wait()
        store.start()
    for _, store in moves:
        store.wait()


def settle(n_cols, slots, y, low, dsum, dinv):
    vmem = pl.BlockSpec(memory_space=pltpu.VMEM)
    smem = pl.BlockSpec(memory_space=pltpu.SMEM)
    anywhere = pl.BlockSpec(memory_space=pl.ANY)
    return pl.pallas_call(
        functools.partial(settle_kernel, n_cols - 1),
        out_shape=tuple(jax.ShapeDtypeStruct(x.shape, F32) for x in (y, low, dinv)),
        in_specs=[smem, anywhere, anywhere, vmem, vmem],
        out_specs=(anywhere, anywhere, vmem),
        scratch_shapes=[
            pltpu.VMEM(y.shape, F32), pltpu.VMEM(low.shape, F32),
            pltpu.SemaphoreType.DMA((24,)), pltpu.SemaphoreType.DMA((24,)),
        ],
        compiler_params=pltpu.CompilerParams(vmem_limit_bytes=66_000_000),
    )(slots, y, low, dsum, dinv)


def shards(inverse_rows, panels, diag_inverse, pattern, owner_slot):
    n_rows, n_cols = lax.axis_size("row"), lax.axis_size("col")
    y, low, dsum = exchange(n_rows, n_cols, inverse_rows, panels[0], pattern, owner_slot)
    y, low, diag = settle(n_cols, owner_slot, y, low, dsum, diag_inverse)
    return low, y, diag


def solution(mesh):
    in_specs = (P("col", "row"), P("col", "row", None), P(), P(), P())
    out_specs = (P(None, "row", None), P(None, None, "col"), P())
    return jax.shard_map(shards, mesh=mesh, in_specs=in_specs, out_specs=out_specs, check_vma=False)
```
